256 devices in a mesh: snap: 4 (over x), dom: 64 (over y, z, core).
Axes of the slice: x: 4, y: 4, z: 8, core: 2. Of those that a mesh axis runs over, the one named last changes fastest.
Arguments:
- readings: bfloat16 [4, 2, 32768], P('snap', None, 'dom'), may hold values from -6 to 6
- previous: bfloat16 [4, 64, 32768], P('snap', None, 'dom'), may hold values from -3 to 3
- upstream: bfloat16 [4, 64, 32768], P('snap', None, 'dom'), may hold values from -6 to 6
- gate_weight: bfloat16 [128, 330], replicated, may hold values from -0.3125 to 0.3125
- gate_bias: float32 [128], replicated, may hold values from -4 to 4
- cand_weight: bfloat16 [64, 330], replicated, may hold values from -0.3125 to 0.3125
- cand_bias: float32 [64], replicated, may hold values from -3 to 3
- neighbours: int32 [4, 32768], P(None, 'dom'), may hold values from 0 to 767, as said below
- edge_weight: float32 [4, 32768], P(None, 'dom'), may hold values from 0.1 to 1
- send_rows: int32 [64, 256], P('dom'), may hold values from 0 to 511, as said below
Outputs:
- state_grad: bfloat16 [4, 64, 32768], P('snap', None, 'dom')
- gate_weight_grad: float32 [128, 330], replicated
- gate_bias_grad: float32 [128], replicated
- cand_weight_grad: float32 [64, 330], replicated
- cand_bias_grad: float32 [64], replicated
The draws below stay inside these ranges and needn't reach their ends.
Inputs may be any that keep to these rules, and one draw needn't show every extreme that they name: Value v of neighbours[d, i] below 512 is a row of segment i's own partition; v = 512 + q * 4 + s names slot s of what partition q sends to segment i's partition. Row d = 0 names each row of a partition exactly once, and in every partition every value from 512 to 767 appears. `send_rows`: row q holds rows of partition q; slots p * 4 to p * 4 + 3 are those sent to partition p; rows may repeat.
All inputs are finite; a program needn't handle non-finite values.
Results may differ from the reference program's by a relative error of at most 0.006.
Values may be sent and summed in bfloat16 or wider, within the bound.
A program may use at most 64 MiB of HBM per device.

```python
import math
import jax
import jax.numpy as jnp
from jax import lax

FIN = 2
H = 64
M = 5
DEG = 4
SEG_DEV = 512
CAP = 4
SNAPS = 4
SEGMENTS = 32768
HALO = 256
N_DOM = 64


def draw_neighbours(key, part):
    keys = jax.random.split(jax.random.fold_in(key, 11), N_DOM)

    def one_part(part_key):
        first_key, order_key, local_key, remote_key, pick_key = jax.random.split(part_key, 5)
        first = jax.random.permutation(first_key, SEG_DEV).astype(jnp.int32)
        order = jax.random.permutation(order_key, SEG_DEV).astype(jnp.int32)
        covered = jnp.zeros((SEG_DEV,), jnp.int32).at[order[:HALO]].set(SEG_DEV + jnp.arange(HALO, dtype=jnp.int32))
        marked = jnp.zeros((SEG_DEV,), jnp.int32).at[order[:HALO]].set(1)
        local = jax.random.randint(local_key, (DEG - 1, SEG_DEV), 0, SEG_DEV, dtype=jnp.int32)
        remote = jax.random.randint(remote_key, (DEG - 1, SEG_DEV), SEG_DEV, SEG_DEV + HALO, dtype=jnp.int32)
        picked = jax.random.randint(pick_key, (DEG - 1, SEG_DEV), 0, 10, dtype=jnp.int32)
        rest = jnp.where(picked == 0, remote, local)
        head = jnp.where(marked == 1, covered, rest[0])
        return jnp.concatenate([first[None, :], head[None, :], rest[1:]], axis=0)
    blocks = jax.vmap(one_part)(keys)
    return jnp.transpose(blocks, (1, 0, 2)).reshape(DEG, SEG_DEV * N_DOM)


def draw_send_rows(key, part):
    rows_key, high_key, low_key = jax.random.split(jax.random.fold_in(key, 7), 3)
    rows = jax.random.randint(rows_key, (N_DOM, HALO), 0, SEG_DEV, dtype=jnp.int32)
    high_spot = jax.random.randint(high_key, (N_DOM,), 0, HALO, dtype=jnp.int32)
    low_spot = (high_spot + 1 + jax.random.randint(low_key, (N_DOM,), 0, HALO - 1, dtype=jnp.int32)) % HALO
    column = jnp.arange(HALO, dtype=jnp.int32)[None, :]
    rows = jnp.where(column == high_spot[:, None], SEG_DEV - 1, rows)
    rows = jnp.where(column == low_spot[:, None], 0, rows)
    return rows.astype(jnp.int32)


def level_of(key, shape, pieces, low, top_value):
    factor_of, own = 1.0, jax.random.fold_in(key, 6)
    for dim, shards_of in pieces:
        draws = jnp.exp(jax.random.uniform(jax.random.fold_in(own, dim), (shards_of,), jnp.float32, low / len(pieces), top_value / len(pieces)))
        factor_of = factor_of * jnp.repeat(draws, shape[dim] // shards_of).reshape([-1 if axis == dim else 1 for axis in range(len(shape))])
    return factor_of


def bell_draw(own_key, shape, width, limit, pieces=(), kind=jnp.bfloat16):
    gain = level_of(own_key, shape, pieces, -0.22, 0.18) if pieces else 1.0
    entries = jax.random.normal(own_key, shape, jnp.float32) * width * gain
    return jnp.minimum(jnp.maximum(entries, -limit), limit).astype(kind)


def setup_inputs(seed: int = 0) -> dict:
    splits = jax.random.split(jax.random.key(seed), 11)
    return {
        "readings": bell_draw(splits[0], (SNAPS, FIN, SEGMENTS), 1.0, 6.0, ((0, 4), (2, 64))),
        "previous": bell_draw(splits[1], (SNAPS, H, SEGMENTS), 0.5, 3.0, ((0, 4), (2, 64))),
        "upstream": bell_draw(splits[2], (SNAPS, H, SEGMENTS), 1.0, 6.0, ((0, 4), (2, 64))),
        "gate_weight": bell_draw(splits[3], (2 * H, M * (FIN + H)), (M * (FIN + H)) ** -0.5, 0.3125),
        "gate_bias": bell_draw(splits[4], (2 * H,), 1.0, 4.0, (), jnp.float32),
        "cand_weight": bell_draw(splits[5], (H, M * (FIN + H)), (M * (FIN + H)) ** -0.5, 0.3125),
        "cand_bias": bell_draw(splits[6], (H,), 0.5, 3.0, (), jnp.float32),
        "neighbours": draw_neighbours(jax.random.fold_in(splits[10], 71), 0),
        "edge_weight": jnp.clip(jnp.exp(math.log(1.0) - 2.3025851 * jax.random.uniform(splits[8], (DEG, SEGMENTS), jnp.float32) ** level_of(splits[8], (DEG, SEGMENTS), ((1, 64),), -0.2, 0.2)), 0.1, 1.0),
        "send_rows": draw_send_rows(jax.random.fold_in(splits[10], 71), 0),
    }


def global_sources(neighbours, send_rows):
    total = neighbours.shape[1]
    node = jnp.arange(total, dtype=jnp.int32)
    owner = (node // SEG_DEV).astype(jnp.int32)
    halo_index = jnp.clip(neighbours - SEG_DEV, 0, HALO - 1).astype(jnp.int32)
    peer = (halo_index // CAP).astype(jnp.int32)
    position = (halo_index % CAP).astype(jnp.int32)
    remote_row = send_rows[peer, owner[None, :] * CAP + position]
    local_src = owner[None, :] * SEG_DEV + neighbours
    remote_src = peer * SEG_DEV + remote_row
    return jnp.where(neighbours < SEG_DEV, local_src, remote_src).astype(jnp.int32)

def collect(values, weights, sources):
    total = jnp.zeros(values.shape, jnp.float32)
    for slot in range(sources.shape[0]):
        total = total + values[:, sources[slot]].astype(jnp.float32) * weights[slot][None, :]
    return total

def spread(values, weights, sources):
    total = jnp.zeros(values.shape, jnp.float32)
    for slot in range(sources.shape[0]):
        total = total.at[:, sources[slot]].add(values.astype(jnp.float32) * weights[slot][None, :])
    return total

def reference(readings, previous, upstream, gate_weight, gate_bias, cand_weight, cand_bias, neighbours, edge_weight, send_rows):
    sources = global_sources(neighbours, send_rows)
    total_rows = neighbours.shape[1]
    in_degree = lax.optimization_barrier(jnp.sum(edge_weight, axis=0))
    out_degree = jnp.zeros((total_rows,), jnp.float32)
    for slot in range(sources.shape[0]):
        out_degree = out_degree.at[sources[slot]].add(edge_weight[slot])
    walk_in = edge_weight / in_degree[None, :]
    walk_out = edge_weight / out_degree[sources]

    def diffuse(base):
        lower = base.astype(jnp.float32)
        first_out = spread(base, walk_out, sources).astype(jnp.bfloat16)
        second_out = (2.0 * spread(first_out, walk_out, sources) - lower).astype(jnp.bfloat16)
        first_in = collect(base, walk_in, sources).astype(jnp.bfloat16)
        second_in = (2.0 * collect(first_in, walk_in, sources) - lower).astype(jnp.bfloat16)
        return jnp.concatenate([base, first_out, second_out, first_in, second_in], axis=0)

    def adjoint(grads):
        pulled = collect(grads[2], walk_out, sources)
        pushed = spread(grads[4], walk_in, sources)
        turned_out = (grads[1].astype(jnp.float32) + 2.0 * pulled).astype(jnp.bfloat16)
        turned_in = (grads[3].astype(jnp.float32) + 2.0 * pushed).astype(jnp.bfloat16)
        direct = grads[0].astype(jnp.float32) - grads[2].astype(jnp.float32) - grads[4].astype(jnp.float32)
        return direct + collect(turned_out, walk_out, sources) + spread(turned_in, walk_in, sources)
    chans = FIN + H
    cand_rows = cand_weight.reshape(H, M, chans)[:, :, FIN:].reshape(H, M * H)
    gate_rows = gate_weight.reshape(2 * H, M, chans)[:, :, FIN:].reshape(2 * H, M * H)
    grad_wru = jnp.zeros((2 * H, M * chans), jnp.float32)
    grad_bru = jnp.zeros((2 * H,), jnp.float32)
    grad_wc = jnp.zeros((H, M * chans), jnp.float32)
    grad_bc = jnp.zeros((H,), jnp.float32)
    results = []
    for snap in range(SNAPS):
        upward = upstream[snap].astype(jnp.float32)
        held = previous[snap].astype(jnp.float32)
        states = diffuse(jnp.concatenate([readings[snap], previous[snap]], axis=0))
        gates = jnp.dot(gate_weight, states, preferred_element_type=jnp.float32) + gate_bias[:, None]
        reset = jax.nn.sigmoid(gates[:H])
        update = jax.nn.sigmoid(gates[H:])
        scaled = (reset * held).astype(jnp.bfloat16)
        mixed = diffuse(jnp.concatenate([readings[snap], scaled], axis=0))
        cand = jnp.tanh(jnp.dot(cand_weight, mixed, preferred_element_type=jnp.float32) + cand_bias[:, None])
        cand_grad = (upward * (1.0 - update) * (1.0 - cand * cand)).astype(jnp.bfloat16)
        grad_wc = grad_wc + jnp.dot(cand_grad, mixed.T, preferred_element_type=jnp.float32)
        grad_bc = grad_bc + lax.optimization_barrier(jnp.sum(cand_grad.astype(jnp.float32), axis=1))
        back_c = jnp.dot(cand_rows.T, cand_grad, preferred_element_type=jnp.float32).astype(jnp.bfloat16).reshape(M, H, total_rows)
        scaled_grad = adjoint(back_c)
        reset_part = scaled_grad * held * reset * (1.0 - reset)
        update_part = upward * (held - cand) * update * (1.0 - update)
        gate_grad = jnp.concatenate([reset_part, update_part], axis=0).astype(jnp.bfloat16)
        grad_wru = grad_wru + jnp.dot(gate_grad, states.T, preferred_element_type=jnp.float32)
        grad_bru = grad_bru + lax.optimization_barrier(jnp.sum(gate_grad.astype(jnp.float32), axis=1))
        back_g = jnp.dot(gate_rows.T, gate_grad, preferred_element_type=jnp.float32).astype(jnp.bfloat16).reshape(M, H, total_rows)
        state_part = adjoint(back_g)
        results.append((upward * update + scaled_grad * reset + state_part).astype(jnp.bfloat16))
    factor = 1.0 / math.sqrt(SNAPS * SEGMENTS)
    state_grad = jnp.stack(results, axis=0)
    return (state_grad, grad_wru * factor, grad_bru * factor, grad_wc * factor, grad_bc * factor)
```

```python
import math

import jax
import jax.numpy as jnp
from jax import lax
from jax.experimental import pallas as pl
from jax.experimental.pallas import tpu as pltpu
from jax.sharding import PartitionSpec as P

F32, BF16 = jnp.float32, jnp.bfloat16
MESH = pl.DeviceIdType.MESH
HOPS = 8


def mm(a, b):
    return jnp.dot(a, b, preferred_element_type=F32)


def turn(a):
    return jnp.transpose(a.astype(F32))


def lanes(rows, width):
    return lax.broadcasted_iota(jnp.int32, (rows, width), 1)


def forward_map(lane, chans, fin):
    tile, at = lane // 128, lane % 128
    upper, low = at >= 64, at % 64
    first = jnp.where(upper, 3 * chans, chans) + fin + low
    second = jnp.where(upper, 4 * chans, 2 * chans) + fin + low
    third = jnp.where(upper, jnp.where(low < fin, low, -1), fin + low)
    order = jnp.where(upper, 3, 1) + low // fin
    fourth = jnp.where(low < 2 * fin, order * chans + low % fin, -1)
    return jnp.where(tile == 0, first, jnp.where(tile == 1, second, jnp.where(tile == 2, third, fourth)))


def backward_map(lane, chans, fin):
    tile, at = lane // 128, lane % 128
    upper, low = at >= 64, at % 64
    order = jnp.where(
        tile == 0, jnp.where(upper, 2, 4), jnp.where(tile == 1, jnp.where(upper, 1, 3), 0)
    )
    return order * chans + fin + low


def kernel(
    n_dom, width, fin, chans, halo,
    readings_ref, previous_ref, upstream_ref, gw_ref, gb_ref, cw_ref, cb_ref, nb_ref, ew_ref, sr_ref,
    state_ref, pg_ref,
    sp, ml, wl, sw, held, upward, scale_f, scale_a, local, wide, states, mixed, field, wg, wc, bg, bc,
    send_w, recv_w, send_n, recv_n, ssem, rsem, osem, rows,
):
    me = lax.axis_index("dom")
    barrier = pltpu.get_barrier_semaphore()

    def peer_of(k):
        return (me + k) % n_dom

    def greet(k, c):
        pl.semaphore_signal(barrier, inc=1, device_id={"dom": peer_of(k)}, device_id_type=MESH)
        return c

    lax.fori_loop(1, n_dom, greet, 0)

    lane128 = lanes(width, 128)
    low128 = lane128 < 64

    prev = previous_ref[0].astype(F32)
    held[...] = jnp.transpose(jnp.concatenate([prev, prev], axis=0))
    ups = upstream_ref[0].astype(F32)
    upward[...] = jnp.transpose(jnp.concatenate([ups, ups], axis=0))
    read = readings_ref[0].astype(F32)
    degs = nb_ref.shape[0]
    rows[...] = jnp.zeros_like(rows)
    rows[0, 0:fin, :] = read
    rows[0, 64 : 64 + fin, :] = read
    rows[1, 0:degs, :] = nb_ref[...].astype(F32)
    rows[1, 8 : 8 + degs, :] = ew_ref[...]
    rows[1, 16:17, :halo] = sr_ref[...].astype(F32)
    extra = jnp.transpose(rows[0])
    columns = jnp.transpose(rows[1])

    rows_sel = columns[:halo, 16:17].astype(jnp.int32)
    sp[:halo, :] = jnp.where(lanes(halo, width) == rows_sel, 1.0, 0.0).astype(BF16)

    def push_block(first, rows):
        here = lax.broadcasted_iota(jnp.int32, (rows, width), 0) + first
        total = jnp.zeros((rows, width), F32)
        for d in range(degs):
            total = total + jnp.where(nb_ref[d : d + 1, :] == here, ew_ref[d : d + 1, :], 0.0)
        return total

    edge_sums = push_block(width, halo)
    sp[halo:, :] = edge_sums.astype(BF16)
    deg_halo = jnp.sum(edge_sums, axis=1, keepdims=True)
    deg_high = deg_halo.astype(BF16).astype(F32)
    deg_rest = deg_halo - deg_high

    def send_buf(hop):
        return send_w.at[hop] if hop < 2 else send_n.at[hop - 2]

    def recv_buf(hop):
        return recv_w.at[hop] if hop < 2 else recv_n.at[hop - 2]

    def launch(hop, values):
        span = values.shape[1]
        mixed_rows = mm(sp[...], values)
        out = jnp.where(
            lanes(halo, span) % 128 < 64, mixed_rows[halo:, :], mixed_rows[:halo, :]
        )
        if hop == 0:
            lane = lanes(halo, span)
            out = jnp.where(lane == 128 + fin, deg_high, jnp.where(lane == 128 + fin + 1, deg_rest, out))
        out = out.astype(BF16)
        src, dst = send_buf(hop), recv_buf(hop)
        for part in range(span // 128):
            src.at[part].reshape(halo, 128)[...] = out[:, part * 128 : part * 128 + 128]

        if hop == 0:
            pl.semaphore_wait(barrier, n_dom - 1)

        def go(k, c):
            pltpu.make_async_remote_copy(
                src.at[:, peer_of(k)], dst.at[:, me], ssem.at[hop], rsem.at[hop],
                device_id={"dom": peer_of(k)}, device_id_type=MESH,
            ).start()
            return c

        lax.fori_loop(1, n_dom, go, 0)
        pltpu.make_async_copy(src.at[:, me], dst.at[:, me], osem.at[hop]).start()

    def near(values):
        span = values.shape[1]
        low = lanes(width, span) % 128 < 64
        return jnp.where(low, mm(ml[...], values), mm(wl[...], values))

    def await_recv(hop):
        src, dst = send_buf(hop), recv_buf(hop)
        pltpu.make_async_copy(
            src.at[:, pl.ds(0, n_dom - 1)], dst.at[:, pl.ds(0, n_dom - 1)], rsem.at[hop]
        ).wait()
        pltpu.make_async_copy(src.at[:, me], dst.at[:, me], osem.at[hop]).wait()

    def far(hop):
        dst = recv_buf(hop)
        span = 256 if hop < 2 else 128
        got = [dst.at[part].reshape(halo, 128)[...] for part in range(span // 128)]
        got = got[0] if len(got) == 1 else jnp.concatenate(got, axis=1)
        both = mm(sw[...], got)
        low = lanes(width, span) % 128 < 64
        return jnp.where(low, both[:width, :], both[width:, :])

    start = jnp.concatenate([held[...], extra], axis=1)
    launch(0, start.astype(BF16))

    wts = [columns[:, 8 + d : 9 + d] for d in range(degs)]
    srcs = [columns[:, d : d + 1].astype(jnp.int32) for d in range(degs)]
    for first in range(0, width, 128):
        here = lanes(128, width + halo)
        total = jnp.zeros((128, width + halo), F32)
        for d in range(degs):
            total = total + jnp.where(srcs[d][first : first + 128] == here, wts[d][first : first + 128], 0.0)
        total = total.astype(BF16)
        wl[first : first + 128, :] = total[:, :width]
        sw[width + first : width + first + 128, :] = total[:, width:]
    deg_near = []
    for first in range(0, width, 128):
        block = push_block(first, 128)
        ml[first : first + 128, :] = block.astype(BF16)
        deg_near.append(jnp.sum(block, axis=1, keepdims=True))
    deg_near = jnp.concatenate(deg_near, axis=0)
    sw[:width, :] = jnp.where(
        lax.broadcasted_iota(jnp.int32, (width, halo), 0) == sr_ref[...], 1.0, 0.0
    ).astype(BF16)
    deg_in = wts[0]
    for d in range(1, degs):
        deg_in = deg_in + wts[d]
    inv_in = 1.0 / deg_in

    cols = gw_ref.shape[1]
    pick = (
        lax.broadcasted_iota(jnp.int32, (cols, 512), 0) == forward_map(lanes(1, 512), chans, fin)
    )
    pick = jnp.where(pick, 1.0, 0.0).astype(BF16)
    pick_b = (
        lax.broadcasted_iota(jnp.int32, (cols, 384), 0) == backward_map(lanes(1, 384), chans, fin)
    )
    pick_b = jnp.where(pick_b, 1.0, 0.0).astype(BF16)
    gate_w = gw_ref[...]
    cand_w = cw_ref[...]
    gate_f = mm(gate_w, pick)
    cand_f = mm(cand_w, pick)
    r, u = gate_f[:64], gate_f[64:]
    wg[...] = jnp.transpose(jnp.concatenate([r, r, u, u], axis=0)).astype(BF16)
    wc[...] = jnp.transpose(jnp.concatenate([cand_f, cand_f], axis=0)).astype(BF16)
    bg[...] = mm(gate_w, pick_b).astype(BF16)
    bc[:64, :] = mm(cand_w, pick_b).astype(BF16)
    bc[64:, :] = jnp.zeros((64, 384), BF16)

    wide[...] = near(start.astype(BF16))
    await_recv(0)
    raw = far(0)
    deg_out = deg_near + raw[:, 128 + fin : 129 + fin] + raw[:, 129 + fin : 130 + fin]
    raw = raw + wide[...]
    inv_out = 1.0 / deg_out
    scale_f[...] = jnp.where(low128, inv_out, inv_in)
    scale_a[...] = jnp.where(low128, inv_in, inv_out)
    first_main = (raw[:, :128] * scale_f[...]).astype(BF16)
    states[:, :128] = first_main
    first_extra = jnp.where(lane128 % 64 < fin, raw[:, 128:] * scale_f[...], 0.0)
    second_in = jnp.concatenate([first_main, first_extra.astype(BF16)], axis=1)
    launch(1, second_in)
    ones = jnp.where(
        low128, held[...], jnp.where(lane128 < 64 + fin, extra, jnp.where(lane128 == 64 + fin, 1.0, 0.0))
    )
    states[:, 256:384] = ones.astype(BF16)
    wide[...] = near(second_in)
    await_recv(1)
    raw = far(1) + wide[...]
    states[:, 128:256] = (2.0 * raw[:, :128] * scale_f[...] - held[...]).astype(BF16)
    second_extra = 2.0 * raw[:, 128:] * scale_f[...] - extra
    tail = first_extra.astype(BF16).astype(F32) + pltpu.roll(second_extra.astype(BF16).astype(F32), fin, 1)
    states[:, 384:] = tail.astype(BF16)

    gates = mm(states[...], wg[...])
    bias = jnp.broadcast_to(gb_ref[...], (width, 128))
    turned = pltpu.roll(bias, 64, 1)
    reset = jax.nn.sigmoid(gates[:, :128] + jnp.where(low128, bias, turned))
    update = jax.nn.sigmoid(gates[:, 128:] + jnp.where(low128, turned, bias))
    scaled = (reset * held[...]).astype(BF16)

    launch(2, scaled)
    mixed[:, 256:384] = jnp.where(low128, scaled, states[:, 256:384])
    mixed[:, 384:] = states[:, 384:]
    local[...] = near(scaled)
    await_recv(2)
    hop_one = ((far(2) + local[...]) * scale_f[...]).astype(BF16)
    launch(3, hop_one)
    mixed[:, :128] = hop_one
    local[...] = near(hop_one)
    await_recv(3)
    raw = far(3) + local[...]
    mixed[:, 128:256] = (2.0 * raw * scale_f[...] - scaled.astype(F32)).astype(BF16)
    cand = jnp.tanh(mm(mixed[...], wc[...]) + cb_ref[...])
    cand_grad = (upward[...] * (1.0 - update) * (1.0 - cand * cand)).astype(BF16)

    def back(grad, weights, hop):
        outer = mm(grad, weights[:, :128])
        values = (outer * scale_a[...]).astype(BF16)
        launch(hop, values)
        local[...] = near(values)
        inner = mm(grad, weights[:, 128:256])
        direct = mm(grad, weights[:, 256:384]) - outer - pltpu.roll(outer, 64, 1)
        field[...] = direct
        await_recv(hop)
        raw = far(hop) + local[...]
        values = ((inner + 2.0 * raw) * scale_a[...]).astype(BF16)
        launch(hop + 1, values)
        local[...] = near(values)
        return values

    def back_end(hop):
        await_recv(hop + 1)
        raw = far(hop + 1) + local[...]
        return field[...] + raw + pltpu.roll(raw, 64, 1)

    back(cand_grad, bc, 4)
    pg_ref[128:, :] = mm(turn(cand_grad)[:64, :].astype(BF16), mixed[...])
    scaled_grad = back_end(4)
    reset_part = scaled_grad * held[...] * reset * (1.0 - reset)
    update_part = upward[...] * (held[...] - cand) * update * (1.0 - update)
    gate_grad = jnp.where(low128, reset_part, update_part).astype(BF16)
    back(gate_grad, bg, 6)
    pg_ref[:128, :] = mm(turn(gate_grad).astype(BF16), states[...])
    state_part = back_end(6)
    result = upward[...] * update + scaled_grad * reset + state_part
    state_ref[0] = jnp.transpose(result)[:64, :].astype(BF16)

    for hop in range(HOPS):
        src, dst = send_buf(hop), recv_buf(hop)
        pltpu.make_async_copy(
            src.at[:, pl.ds(0, n_dom - 1)], dst.at[:, pl.ds(0, n_dom - 1)], ssem.at[hop]
        ).wait()


def unpermute(grads, chans, fin):
    starts = {1: 0, 3: 64, 2: 128, 4: 192, 0: 256}
    reads = {0: 320, 1: 384, 2: 384 + fin, 3: 448, 4: 448 + fin}
    parts = []
    for m in range(5):
        parts.append(grads[:, reads[m] : reads[m] + fin])
        parts.append(grads[:, starts[m] : starts[m] + chans - fin])
    return jnp.concatenate(parts, axis=1), grads[:, 320 + fin]


def solution(mesh):
    n_dom = mesh.shape["dom"]

    def body(readings, previous, upstream, gw, gb, cw, cb, nb, ew, sr):
        fin, hidden, width = readings.shape[1], previous.shape[1], readings.shape[2]
        chans, halo = fin + hidden, sr.shape[1]
        slots = halo // n_dom
        vmem = pl.BlockSpec(memory_space=pltpu.VMEM)

        def run(*refs):
            kernel(n_dom, width, fin, chans, halo, *refs)

        state, grads = pl.pallas_call(
            run,
            out_shape=(
                jax.ShapeDtypeStruct((1, hidden, width), BF16),
                jax.ShapeDtypeStruct((192, 512), F32),
            ),
            in_specs=[vmem] * 10,
            out_specs=(vmem, vmem),
            scratch_shapes=[
                pltpu.VMEM((2 * halo, width), BF16),
                pltpu.VMEM((width, width), BF16),
                pltpu.VMEM((width, width), BF16),
                pltpu.VMEM((2 * width, halo), BF16),
                pltpu.VMEM((width, 128), F32),
                pltpu.VMEM((width, 128), F32),
                pltpu.VMEM((width, 128), F32),
                pltpu.VMEM((width, 128), F32),
                pltpu.VMEM((width, 128), F32),
                pltpu.VMEM((width, 256), F32),
                pltpu.VMEM((width, 512), BF16),
                pltpu.VMEM((width, 512), BF16),
                pltpu.VMEM((width, 128), F32),
                pltpu.VMEM((512, 256), BF16),
                pltpu.VMEM((512, 128), BF16),
                pltpu.VMEM((128, 384), BF16),
                pltpu.VMEM((128, 384), BF16),
                pltpu.VMEM((2, 2, n_dom, slots, 128), BF16),
                pltpu.VMEM((2, 2, n_dom, slots, 128), BF16),
                pltpu.VMEM((HOPS - 2, 1, n_dom, slots, 128), BF16),
                pltpu.VMEM((HOPS - 2, 1, n_dom, slots, 128), BF16),
                pltpu.SemaphoreType.DMA((HOPS,)),
                pltpu.SemaphoreType.DMA((HOPS,)),
                pltpu.SemaphoreType.DMA((HOPS,)),
                pltpu.VMEM((2, 128, width), F32),
            ],
            compiler_params=pltpu.CompilerParams(collective_id=0, has_side_effects=True),
        )(readings, previous, upstream, gw, gb.reshape(1, -1), cw, jnp.tile(cb.reshape(1, -1), (1, 2)), nb, ew, sr)
        factor = 1.0 / math.sqrt(readings.shape[0] * lax.axis_size("snap") * width * n_dom)
        grads = lax.psum(grads, ("snap", "dom")) * factor
        all_w, all_b = unpermute(grads, chans, fin)
        return state, all_w[:128], all_b[:128], all_w[128:], all_b[128:]

    in_specs = (
        P("snap", None, "dom"), P("snap", None, "dom"), P("snap", None, "dom"),
        P(), P(), P(), P(), P(None, "dom"), P(None, "dom"), P("dom", None),
    )
    out_specs = (P("snap", None, "dom"), P(), P(), P(), P())
    return jax.shard_map(body, mesh=mesh, in_specs=in_specs, out_specs=out_specs, check_vma=False)
```

```python
import math

import jax
import jax.numpy as jnp
from jax import lax
from jax.experimental import pallas as pl
from jax.experimental.pallas import tpu as pltpu
from jax.sharding import PartitionSpec as P

F32, BF16 = jnp.float32, jnp.bfloat16
MESH = pl.DeviceIdType.MESH
HOPS = 8
RS_EARLY, AG_EARLY, RS_LATE, AG_LATE, GROUPS = 8, 9, 10, 11, 12


def mm(a, b):
    return jnp.dot(a, b, preferred_element_type=F32)


def turn(a):
    return jnp.transpose(a.astype(F32))


def lanes(rows, width):
    return lax.broadcasted_iota(jnp.int32, (rows, width), 1)


def forward_map(lane, chans, fin):
    tile, at = lane // 128, lane % 128
    upper, low = at >= 64, at % 64
    first = jnp.where(upper, 3 * chans, chans) + fin + low
    second = jnp.where(upper, 4 * chans, 2 * chans) + fin + low
    third = jnp.where(upper, jnp.where(low < fin, low, -1), fin + low)
    order = jnp.where(upper, 3, 1) + low // fin
    fourth = jnp.where(low < 2 * fin, order * chans + low % fin, -1)
    return jnp.where(tile == 0, first, jnp.where(tile == 1, second, jnp.where(tile == 2, third, fourth)))


def backward_map(lane, chans, fin):
    tile, at = lane // 128, lane % 128
    upper, low = at >= 64, at % 64
    order = jnp.where(
        tile == 0, jnp.where(upper, 2, 4), jnp.where(tile == 1, jnp.where(upper, 1, 3), 0)
    )
    return order * chans + fin + low


def kernel(
    n_dom, n_snap, width, fin, chans, halo, factor,
    readings_ref, previous_ref, upstream_ref, gw_ref, gb_ref, cw_ref, cb_ref, nb_ref, ew_ref, sr_ref,
    state_ref, gate_out, gate_bias_out, cand_out, cand_bias_out,
    sp, ml, wl, sw, held, upward, scale_f, scale_a, local, wide, states, mixed, field, wg, wc, bg, bc,
    send_w, recv_w, send_n, recv_n, ssem, rsem, osem, rows,
    early, late, piece_e, piece_l, snap_send, snap_recv, snap_s, snap_r, back_pick,
):
    me = lax.axis_index("dom")
    barrier = pltpu.get_barrier_semaphore()

    def peer_of(k):
        return (me + k) % n_dom

    def greet(k, c):
        pl.semaphore_signal(barrier, inc=1, device_id={"dom": peer_of(k)}, device_id_type=MESH)
        return c

    lax.fori_loop(1, n_dom, greet, 0)
    mine = lax.axis_index("snap")
    for k in range(1, n_snap):
        pl.semaphore_signal(barrier, inc=1, device_id={"snap": (mine + k) % n_snap}, device_id_type=MESH)

    lane128 = lanes(width, 128)
    low128 = lane128 < 64

    prev = previous_ref[0].astype(F32)
    held[...] = jnp.transpose(jnp.concatenate([prev, prev], axis=0))
    ups = upstream_ref[0].astype(F32)
    upward[...] = jnp.transpose(jnp.concatenate([ups, ups], axis=0))
    read = readings_ref[0].astype(F32)
    degs = nb_ref.shape[0]
    rows[...] = jnp.zeros_like(rows)
    rows[0, 0:fin, :] = read
    rows[0, 64 : 64 + fin, :] = read
    rows[1, 0:degs, :] = nb_ref[...].astype(F32)
    rows[1, 8 : 8 + degs, :] = ew_ref[...]
    rows[1, 16:17, :halo] = sr_ref[...].astype(F32)
    extra = jnp.transpose(rows[0])
    columns = jnp.transpose(rows[1])

    rows_sel = columns[:halo, 16:17].astype(jnp.int32)
    sp[:halo, :] = jnp.where(lanes(halo, width) == rows_sel, 1.0, 0.0).astype(BF16)

    def push_block(first, rows):
        here = lax.broadcasted_iota(jnp.int32, (rows, width), 0) + first
        total = jnp.zeros((rows, width), F32)
        for d in range(degs):
            total = total + jnp.where(nb_ref[d : d + 1, :] == here, ew_ref[d : d + 1, :], 0.0)
        return total

    edge_sums = push_block(width, halo)
    sp[halo:, :] = edge_sums.astype(BF16)
    deg_halo = jnp.sum(edge_sums, axis=1, keepdims=True)
    deg_high = deg_halo.astype(BF16).astype(F32)
    deg_rest = deg_halo - deg_high

    def send_buf(hop):
        if hop >= HOPS:
            return {RS_EARLY: early.at[0], RS_LATE: late.at[0]}[hop]
        return send_w.at[hop] if hop < 2 else send_n.at[hop - 2]

    def recv_buf(hop):
        if hop >= HOPS:
            return {RS_EARLY: early.at[1], AG_EARLY: early.at[2], RS_LATE: late.at[1], AG_LATE: late.at[2]}[hop]
        return recv_w.at[hop] if hop < 2 else recv_n.at[hop - 2]

    def send_all(group):
        src, dst = send_buf(group), recv_buf(group)

        def go(k, c):
            pltpu.make_async_remote_copy(
                src.at[:, peer_of(k)], dst.at[:, me], ssem.at[group], rsem.at[group],
                device_id={"dom": peer_of(k)}, device_id_type=MESH,
            ).start()
            return c

        lax.fori_loop(1, n_dom, go, 0)
        pltpu.make_async_copy(src.at[:, me], dst.at[:, me], osem.at[group]).start()

    def spread_piece(group, src):
        dst = recv_buf(group)

        def go(k, c):
            pltpu.make_async_remote_copy(
                src, dst.at[:, me], ssem.at[group], rsem.at[group],
                device_id={"dom": peer_of(k)}, device_id_type=MESH,
            ).start()
            return c

        lax.fori_loop(1, n_dom, go, 0)
        pltpu.make_async_copy(src, dst.at[:, me], osem.at[group]).start()

    def launch(hop, values):
        span = values.shape[1]
        mixed_rows = mm(sp[...], values)
        out = jnp.where(
            lanes(halo, span) % 128 < 64, mixed_rows[halo:, :], mixed_rows[:halo, :]
        )
        if hop == 0:
            lane = lanes(halo, span)
            out = jnp.where(lane == 128 + fin, deg_high, jnp.where(lane == 128 + fin + 1, deg_rest, out))
        out = out.astype(BF16)
        src = send_buf(hop)
        for part in range(span // 128):
            src.at[part].reshape(halo, 128)[...] = out[:, part * 128 : part * 128 + 128]

        if hop == 0:
            pl.semaphore_wait(barrier, n_dom + n_snap - 2)
        send_all(hop)

    def near(values):
        span = values.shape[1]
        low = lanes(width, span) % 128 < 64
        return jnp.where(low, mm(ml[...], values), mm(wl[...], values))

    def await_recv(hop):
        dst = recv_buf(hop)
        rest = dst.at[:, pl.ds(0, n_dom - 1)]
        pltpu.make_async_copy(rest, rest, rsem.at[hop]).wait()
        pltpu.make_async_copy(dst.at[:, me], dst.at[:, me], osem.at[hop]).wait()

    def reduce_pieces(group, which):
        await_recv(group)
        dst = recv_buf(group)
        parts = dst.shape[0]
        row = lax.broadcasted_iota(jnp.int32, (8, halo * parts), 0)
        col = lanes(8, halo * parts)
        slots = dst.shape[2]
        chosen = (col % slots == row % slots) & (col // halo == (row // slots) % parts)
        chosen = jnp.where(chosen, 1.0, 0.0).astype(BF16)
        terms = [dst.at[part].reshape(halo, 128)[...] for part in range(parts)]
        total = mm(chosen[:, :halo], terms[0])
        for part in range(1, parts):
            total = total + mm(chosen[:, part * halo : part * halo + halo], terms[part])
        snap_send[which] = total
        snap_recv[which, mine] = total
        for k in range(1, n_snap):
            pltpu.make_async_remote_copy(
                snap_send.at[which], snap_recv.at[which, mine], snap_s.at[which], snap_r.at[which],
                device_id={"snap": (mine + k) % n_snap}, device_id_type=MESH,
            ).start()

    def finish_pieces(group, which, piece):
        others = snap_recv.at[which, pl.ds(0, n_snap - 1)]
        pltpu.make_async_copy(others, others, snap_r.at[which]).wait()
        total = snap_recv[which, 0]
        for k in range(1, n_snap):
            total = total + snap_recv[which, k]
        slots = piece.shape[1]
        for part in range(piece.shape[0]):
            piece[part] = total[part * slots : (part + 1) * slots, :].astype(BF16)
        spread_piece(group, piece)

    def gathered(group, tile, count):
        at = tile * count
        return recv_buf(group).at[at // halo].reshape(halo, 128)[at % halo : at % halo + count, :]

    def far(hop):
        dst = recv_buf(hop)
        span = 256 if hop < 2 else 128
        got = [dst.at[part].reshape(halo, 128)[...] for part in range(span // 128)]
        got = got[0] if len(got) == 1 else jnp.concatenate(got, axis=1)
        both = mm(sw[...], got)
        low = lanes(width, span) % 128 < 64
        return jnp.where(low, both[:width, :], both[width:, :])

    start = jnp.concatenate([held[...], extra], axis=1)
    launch(0, start.astype(BF16))

    wts = [columns[:, 8 + d : 9 + d] for d in range(degs)]
    srcs = [columns[:, d : d + 1].astype(jnp.int32) for d in range(degs)]
    for first in range(0, width, 128):
        here = lanes(128, width + halo)
        total = jnp.zeros((128, width + halo), F32)
        for d in range(degs):
            total = total + jnp.where(srcs[d][first : first + 128] == here, wts[d][first : first + 128], 0.0)
        total = total.astype(BF16)
        wl[first : first + 128, :] = total[:, :width]
        sw[width + first : width + first + 128, :] = total[:, width:]
    deg_near = []
    for first in range(0, width, 128):
        block = push_block(first, 128)
        ml[first : first + 128, :] = block.astype(BF16)
        deg_near.append(jnp.sum(block, axis=1, keepdims=True))
    deg_near = jnp.concatenate(deg_near, axis=0)
    sw[:width, :] = jnp.where(
        lax.broadcasted_iota(jnp.int32, (width, halo), 0) == sr_ref[...], 1.0, 0.0
    ).astype(BF16)
    deg_in = wts[0]
    for d in range(1, degs):
        deg_in = deg_in + wts[d]
    inv_in = 1.0 / deg_in

    cols = gw_ref.shape[1]
    pick = (
        lax.broadcasted_iota(jnp.int32, (cols, 512), 0) == forward_map(lanes(1, 512), chans, fin)
    )
    pick = jnp.where(pick, 1.0, 0.0).astype(BF16)
    pick_b = (
        lax.broadcasted_iota(jnp.int32, (cols, 384), 0) == backward_map(lanes(1, 384), chans, fin)
    )
    pick_b = jnp.where(pick_b, 1.0, 0.0).astype(BF16)
    column = lax.broadcasted_iota(jnp.int32, (512, 1), 0)
    back_pick[...] = jnp.where(
        lanes(512, 384) == forward_map(column, chans, fin), 1.0, 0.0
    ).astype(BF16)
    gate_w = gw_ref[...]
    cand_w = cw_ref[...]
    gate_f = mm(gate_w, pick)
    cand_f = mm(cand_w, pick)
    r, u = gate_f[:64], gate_f[64:]
    wg[...] = jnp.transpose(jnp.concatenate([r, r, u, u], axis=0)).astype(BF16)
    wc[...] = jnp.transpose(jnp.concatenate([cand_f, cand_f], axis=0)).astype(BF16)
    bg[...] = mm(gate_w, pick_b).astype(BF16)
    bc[:64, :] = mm(cand_w, pick_b).astype(BF16)
    bc[64:, :] = jnp.zeros((64, 384), BF16)

    wide[...] = near(start.astype(BF16))
    await_recv(0)
    raw = far(0)
    deg_out = deg_near + raw[:, 128 + fin : 129 + fin] + raw[:, 129 + fin : 130 + fin]
    raw = raw + wide[...]
    inv_out = 1.0 / deg_out
    scale_f[...] = jnp.where(low128, inv_out, inv_in)
    scale_a[...] = jnp.where(low128, inv_in, inv_out)
    first_main = (raw[:, :128] * scale_f[...]).astype(BF16)
    states[:, :128] = first_main
    first_extra = jnp.where(lane128 % 64 < fin, raw[:, 128:] * scale_f[...], 0.0)
    second_in = jnp.concatenate([first_main, first_extra.astype(BF16)], axis=1)
    launch(1, second_in)
    ones = jnp.where(
        low128, held[...], jnp.where(lane128 < 64 + fin, extra, jnp.where(lane128 == 64 + fin, 1.0, 0.0))
    )
    states[:, 256:384] = ones.astype(BF16)
    wide[...] = near(second_in)
    await_recv(1)
    raw = far(1) + wide[...]
    states[:, 128:256] = (2.0 * raw[:, :128] * scale_f[...] - held[...]).astype(BF16)
    second_extra = 2.0 * raw[:, 128:] * scale_f[...] - extra
    tail = first_extra.astype(BF16).astype(F32) + pltpu.roll(second_extra.astype(BF16).astype(F32), fin, 1)
    states[:, 384:] = tail.astype(BF16)

    gates = mm(states[...], wg[...])
    bias = jnp.broadcast_to(gb_ref[...], (width, 128))
    turned = pltpu.roll(bias, 64, 1)
    reset = jax.nn.sigmoid(gates[:, :128] + jnp.where(low128, bias, turned))
    update = jax.nn.sigmoid(gates[:, 128:] + jnp.where(low128, turned, bias))
    scaled = (reset * held[...]).astype(BF16)

    launch(2, scaled)
    mixed[:, 256:384] = jnp.where(low128, scaled, states[:, 256:384])
    mixed[:, 384:] = states[:, 384:]
    local[...] = near(scaled)
    await_recv(2)
    hop_one = ((far(2) + local[...]) * scale_f[...]).astype(BF16)
    launch(3, hop_one)
    mixed[:, :128] = hop_one
    local[...] = near(hop_one)
    await_recv(3)
    raw = far(3) + local[...]
    mixed[:, 128:256] = (2.0 * raw * scale_f[...] - scaled.astype(F32)).astype(BF16)
    cand = jnp.tanh(mm(mixed[...], wc[...]) + cb_ref[...])
    cand_grad = (upward[...] * (1.0 - update) * (1.0 - cand * cand)).astype(BF16)

    update_part = upward[...] * (held[...] - cand) * update * (1.0 - update)

    def outer_hop(grad, weights, hop):
        outer = mm(grad, weights[:, :128])
        values = (outer * scale_a[...]).astype(BF16)
        launch(hop, values)
        return outer, values

    def inner_hop(grad, weights, hop, outer, values, meanwhile):
        local[...] = near(values)
        inner = mm(grad, weights[:, 128:256])
        field[...] = mm(grad, weights[:, 256:384]) - outer - pltpu.roll(outer, 64, 1)
        meanwhile()
        await_recv(hop)
        raw = far(hop) + local[...]
        values = ((inner + 2.0 * raw) * scale_a[...]).astype(BF16)
        launch(hop + 1, values)
        local[...] = near(values)

    def last_hop(hop):
        await_recv(hop)
        raw = far(hop) + local[...]
        return field[...] + raw + pltpu.roll(raw, 64, 1)

    def early_sums():
        grads = turn(jnp.where(low128, cand_grad.astype(F32), update_part)).astype(BF16)
        by_cand = mm(grads[:64, :], mixed[...])
        by_update = mm(grads[64:, :], states[...])
        for tile in range(4):
            dst = early.at[0, tile // 2].reshape(halo, 128)
            at = tile % 2 * 128
            dst[at : at + 64, :] = by_cand[:, tile * 128 : tile * 128 + 128].astype(BF16)
            dst[at + 64 : at + 128, :] = by_update[:, tile * 128 : tile * 128 + 128].astype(BF16)
        send_all(RS_EARLY)

    outer, values = outer_hop(cand_grad, bc, 4)
    inner_hop(cand_grad, bc, 4, outer, values, early_sums)
    reduce_pieces(RS_EARLY, 0)
    scaled_grad = last_hop(5)
    reset_part = scaled_grad * held[...] * reset * (1.0 - reset)
    gate_grad = jnp.where(low128, reset_part, update_part).astype(BF16)
    outer, values = outer_hop(gate_grad, bg, 6)
    by_reset = mm(turn(gate_grad)[:64, :].astype(BF16), states[...])
    for tile in range(4):
        late.at[0, 0].reshape(halo, 128)[tile * 64 : tile * 64 + 64, :] = by_reset[
            :, tile * 128 : tile * 128 + 128
        ].astype(BF16)
    send_all(RS_LATE)
    inner_hop(gate_grad, bg, 6, outer, values, lambda: finish_pieces(AG_EARLY, 0, piece_e))
    reduce_pieces(RS_LATE, 1)
    finish_pieces(AG_LATE, 1, piece_l)

    await_recv(AG_EARLY)
    bias_row = jnp.where(lanes(8, 128) == 64 + fin, 1.0, 0.0).astype(BF16)

    def put(tiles, weight_out, bias_out):
        total = mm(tiles[0], back_pick[:128, :])
        for tile in range(1, 4):
            total = total + mm(tiles[tile], back_pick[tile * 128 : tile * 128 + 128, :])
        weight_out[...] = total[:, : weight_out.shape[1]] * factor
        bias = lax.dot_general(bias_row, tiles[2], (((1,), (1,)), ((), ())), preferred_element_type=F32)
        bias_out[...] = bias[0:1, :] * factor

    put([gathered(AG_EARLY, tile, 128)[:64] for tile in range(4)], cand_out, cand_bias_out)
    state_part = last_hop(7)
    result = upward[...] * update + scaled_grad * reset + state_part
    state_ref[0] = jnp.transpose(result)[:64, :].astype(BF16)
    await_recv(AG_LATE)
    put(
        [
            jnp.concatenate([gathered(AG_LATE, tile, 64), gathered(AG_EARLY, tile, 128)[64:]], axis=0)
            for tile in range(4)
        ],
        gate_out, gate_bias_out,
    )

    for group in range(GROUPS):
        rest = recv_buf(group).at[:, pl.ds(0, n_dom - 1)]
        pltpu.make_async_copy(rest, rest, ssem.at[group]).wait()
    for which in range(2):
        others = snap_recv.at[which, pl.ds(0, n_snap - 1)]
        pltpu.make_async_copy(others, others, snap_s.at[which]).wait()


def solution(mesh):
    n_dom, n_snap = mesh.shape["dom"], mesh.shape["snap"]

    def body(readings, previous, upstream, gw, gb, cw, cb, nb, ew, sr):
        fin, hidden, width = readings.shape[1], previous.shape[1], readings.shape[2]
        chans, halo = fin + hidden, sr.shape[1]
        slots = halo // n_dom
        vmem = pl.BlockSpec(memory_space=pltpu.VMEM)

        factor = 1.0 / math.sqrt(readings.shape[0] * n_snap * width * n_dom)

        def run(*refs):
            kernel(n_dom, n_snap, width, fin, chans, halo, factor, *refs)

        cols = gw.shape[1]
        state, gate, gate_b, cand, cand_b = pl.pallas_call(
            run,
            out_shape=(
                jax.ShapeDtypeStruct((1, hidden, width), BF16),
                jax.ShapeDtypeStruct((2 * hidden, cols), F32),
                jax.ShapeDtypeStruct((1, 2 * hidden), F32),
                jax.ShapeDtypeStruct((hidden, cols), F32),
                jax.ShapeDtypeStruct((1, hidden), F32),
            ),
            in_specs=[vmem] * 10,
            out_specs=(vmem,) * 5,
            scratch_shapes=[
                pltpu.VMEM((2 * halo, width), BF16),
                pltpu.VMEM((width, width), BF16),
                pltpu.VMEM((width, width), BF16),
                pltpu.VMEM((2 * width, halo), BF16),
                pltpu.VMEM((width, 128), F32),
                pltpu.VMEM((width, 128), F32),
                pltpu.VMEM((width, 128), F32),
                pltpu.VMEM((width, 128), F32),
                pltpu.VMEM((width, 128), F32),
                pltpu.VMEM((width, 256), F32),
                pltpu.VMEM((width, 512), BF16),
                pltpu.VMEM((width, 512), BF16),
                pltpu.VMEM((width, 128), F32),
                pltpu.VMEM((512, 256), BF16),
                pltpu.VMEM((512, 128), BF16),
                pltpu.VMEM((128, 384), BF16),
                pltpu.VMEM((128, 384), BF16),
                pltpu.VMEM((2, 2, n_dom, slots, 128), BF16),
                pltpu.VMEM((2, 2, n_dom, slots, 128), BF16),
                pltpu.VMEM((HOPS - 2, 1, n_dom, slots, 128), BF16),
                pltpu.VMEM((HOPS - 2, 1, n_dom, slots, 128), BF16),
                pltpu.SemaphoreType.DMA((GROUPS,)),
                pltpu.SemaphoreType.DMA((GROUPS,)),
                pltpu.SemaphoreType.DMA((GROUPS,)),
                pltpu.VMEM((2, 128, width), F32),
                pltpu.VMEM((3, 2, n_dom, slots, 128), BF16),
                pltpu.VMEM((3, 1, n_dom, slots, 128), BF16),
                pltpu.VMEM((2, slots, 128), BF16),
                pltpu.VMEM((1, slots, 128), BF16),
                pltpu.VMEM((2, 8, 128), F32),
                pltpu.VMEM((2, n_snap, 8, 128), F32),
                pltpu.SemaphoreType.DMA((2,)),
                pltpu.SemaphoreType.DMA((2,)),
                pltpu.VMEM((512, 384), BF16),
            ],
            compiler_params=pltpu.CompilerParams(collective_id=0, has_side_effects=True),
        )(readings, previous, upstream, gw, gb.reshape(1, -1), cw, jnp.tile(cb.reshape(1, -1), (1, 2)), nb, ew, sr)
        return state, gate, gate_b.reshape(-1), cand, cand_b.reshape(-1)

    in_specs = (
        P("snap", None, "dom"), P("snap", None, "dom"), P("snap", None, "dom"),
        P(), P(), P(), P(), P(None, "dom"), P(None, "dom"), P("dom", None),
    )
    out_specs = (P("snap", None, "dom"), P(), P(), P(), P())
    return jax.shard_map(body, mesh=mesh, in_specs=in_specs, out_specs=out_specs, check_vma=False)
```

```python
import math

import jax
import jax.numpy as jnp
from jax import lax
from jax.experimental import pallas as pl
from jax.experimental.pallas import tpu as pltpu
from jax.sharding import PartitionSpec as P

F32, BF16 = jnp.float32, jnp.bfloat16
MESH = pl.DeviceIdType.MESH
HOPS = 8
RS_EARLY, AG_EARLY, RS_LATE, AG_LATE, GROUPS = 8, 9, 10, 11, 12
NY, NZ, NC = 4, 8, 2


def mm(a, b):
    return jnp.dot(a, b, preferred_element_type=F32)


def mm_t1(a, b):
    return lax.dot_general(a, b, (((1,), (1,)), ((), ())), preferred_element_type=F32)


def turn(a):
    return jnp.transpose(a.astype(F32))


def lanes(rows, width):
    return lax.broadcasted_iota(jnp.int32, (rows, width), 1)


def forward_map(lane, chans, fin):
    tile, at = lane // 128, lane % 128
    upper, low = at >= 64, at % 64
    first = jnp.where(upper, 3 * chans, chans) + fin + low
    second = jnp.where(upper, 4 * chans, 2 * chans) + fin + low
    third = jnp.where(upper, jnp.where(low < fin, low, -1), fin + low)
    order = jnp.where(upper, 3, 1) + low // fin
    fourth = jnp.where(low < 2 * fin, order * chans + low % fin, -1)
    return jnp.where(tile == 0, first, jnp.where(tile == 1, second, jnp.where(tile == 2, third, fourth)))


def backward_map(lane, chans, fin):
    tile, at = lane // 128, lane % 128
    upper, low = at >= 64, at % 64
    order = jnp.where(
        tile == 0, jnp.where(upper, 2, 4), jnp.where(tile == 1, jnp.where(upper, 1, 3), 0)
    )
    return order * chans + fin + low


def kernel(
    n_dom, n_snap, width, fin, chans, halo, factor,
    *refs,
):
    sources, refs = refs[:10], refs[10:]
    landed, refs = refs[-11:-1], refs[:-11] + refs[-1:]
    copies = [
        pltpu.make_async_copy(src, dst, refs[-1].at[at]) for at, (src, dst) in enumerate(zip(sources, landed))
    ]
    for copy in copies:
        copy.start()
    step(n_dom, n_snap, width, fin, chans, halo, factor, copies, *landed, *refs[:-1])


def step(
    n_dom, n_snap, width, fin, chans, halo, factor, copies,
    readings_ref, previous_ref, upstream_ref, gw_ref, gb_ref, cw_ref, cb_ref, nb_ref, ew_ref, sr_ref,
    state_ref, gate_out, gate_bias_out, cand_out, cand_bias_out,
    sp, ml, wl, sw, held, upward, scale_f, scale_a, local, wide, states, mixed, field, wg, wc, bg, bc,
    send_w, recv_w, send_n, recv_n, ssem, rsem, osem, rows,
    early, late, piece_e, piece_l, snap_send, snap_recv, snap_s, snap_r, back_pick, pick, bias2,
):
    me = lax.axis_index("dom")
    barrier = pltpu.get_barrier_semaphore()

    my_core, my_z, my_y = me % NC, me // NC % NZ, me // (NC * NZ)

    def each_peer(visit):
        def ring(t, c):
            z = (my_z + NZ + NZ // 2 + (t + 1) // 2 * (1 - t % 2 * 2)) % NZ
            for dy in (2, 1, 3, 0):
                for dc in range(NC):
                    visit(((my_y + dy) % NY * NZ + z) * NC + (my_core + dc) % NC)
            return c

        lax.fori_loop(0, NZ - 1, ring, 0)
        for dy in (2, 1, 3, 0):
            for dc in range(NC):
                if dy or dc:
                    visit(((my_y + dy) % NY * NZ + my_z) * NC + (my_core + dc) % NC)

    each_peer(lambda peer: pl.semaphore_signal(barrier, inc=1, device_id={"dom": peer}, device_id_type=MESH))
    mine = lax.axis_index("snap")
    for k in range(1, n_snap):
        pl.semaphore_signal(barrier, inc=1, device_id={"snap": (mine + k) % n_snap}, device_id_type=MESH)

    for copy in copies:
        copy.wait()
    lane128 = lanes(width, 128)
    low128 = lane128 < 64

    prev = previous_ref[0].astype(F32)
    held[...] = jnp.transpose(jnp.concatenate([prev, prev], axis=0))
    ups = upstream_ref[0].astype(F32)
    upward[...] = jnp.transpose(jnp.concatenate([ups, ups], axis=0))
    read = readings_ref[0].astype(F32)
    degs = nb_ref.shape[0]
    rows[...] = jnp.zeros_like(rows)
    rows[0, 0:fin, :] = read
    rows[0, 64 : 64 + fin, :] = read
    rows[1, 0:degs, :] = nb_ref[...].astype(F32)
    rows[1, 8 : 8 + degs, :] = ew_ref[...]
    rows[1, 16:17, :halo] = sr_ref[...].astype(F32)
    extra = jnp.transpose(rows[0])
    columns = jnp.transpose(rows[1])

    rows_sel = columns[:halo, 16:17].astype(jnp.int32)
    sp[:halo, :] = jnp.where(lanes(halo, width) == rows_sel, 1.0, 0.0).astype(BF16)

    def push_block(first, rows):
        here = lax.broadcasted_iota(jnp.int32, (rows, width), 0) + first
        total = jnp.zeros((rows, width), F32)
        for d in range(degs):
            total = total + jnp.where(nb_ref[d : d + 1, :] == here, ew_ref[d : d + 1, :], 0.0)
        return total

    edge_sums = push_block(width, halo)
    sp[halo:, :] = edge_sums.astype(BF16)
    deg_halo = jnp.sum(edge_sums, axis=1, keepdims=True)
    deg_high = deg_halo.astype(BF16).astype(F32)
    deg_rest = deg_halo - deg_high

    def send_buf(hop):
        if hop >= HOPS:
            return {RS_EARLY: early.at[0], RS_LATE: late.at[0]}[hop]
        return send_w.at[hop] if hop < 2 else send_n.at[hop - 2]

    def recv_buf(hop):
        if hop >= HOPS:
            return {RS_EARLY: early.at[1], AG_EARLY: early.at[2], RS_LATE: late.at[1], AG_LATE: late.at[2]}[hop]
        return recv_w.at[hop] if hop < 2 else recv_n.at[hop - 2]

    def send_all(group):
        src, dst = send_buf(group), recv_buf(group)

        def go(peer):
            pltpu.make_async_remote_copy(
                src.at[:, peer], dst.at[:, me], ssem.at[group], rsem.at[group],
                device_id={"dom": peer}, device_id_type=MESH,
            ).start()

        each_peer(go)
        pltpu.make_async_copy(src.at[:, me], dst.at[:, me], osem.at[group]).start()

    def spread_piece(group, src):
        dst = recv_buf(group)

        def go(peer):
            pltpu.make_async_remote_copy(
                src, dst.at[:, me], ssem.at[group], rsem.at[group],
                device_id={"dom": peer}, device_id_type=MESH,
            ).start()

        each_peer(go)
        pltpu.make_async_copy(src, dst.at[:, me], osem.at[group]).start()

    def launch(hop, values):
        span = values.shape[1]
        mixed_rows = mm(sp[...], values)
        out = jnp.where(
            lanes(halo, span) % 128 < 64, mixed_rows[halo:, :], mixed_rows[:halo, :]
        )
        if hop == 0:
            lane = lanes(halo, span)
            out = jnp.where(lane == 128 + fin, deg_high, jnp.where(lane == 128 + fin + 1, deg_rest, out))
        out = out.astype(BF16)
        src = send_buf(hop)
        for part in range(span // 128):
            src.at[part].reshape(halo, 128)[...] = out[:, part * 128 : part * 128 + 128]

        if hop == 0:
            pl.semaphore_wait(barrier, n_dom + n_snap - 2)
        send_all(hop)

    def near(values):
        span = values.shape[1]
        low = lanes(width, span) % 128 < 64
        return jnp.where(low, mm(ml[...], values), mm(wl[...], values))

    def await_recv(hop):
        dst = recv_buf(hop)
        rest = dst.at[:, pl.ds(0, n_dom - 1)]
        pltpu.make_async_copy(rest, rest, rsem.at[hop]).wait()
        pltpu.make_async_copy(dst.at[:, me], dst.at[:, me], osem.at[hop]).wait()

    def reduce_pieces(group, which):
        await_recv(group)
        dst = recv_buf(group)
        parts = dst.shape[0]
        row = lax.broadcasted_iota(jnp.int32, (8, halo * parts), 0)
        col = lanes(8, halo * parts)
        slots = dst.shape[2]
        chosen = (col % slots == row % slots) & (col // halo == (row // slots) % parts)
        chosen = jnp.where(chosen, 1.0, 0.0).astype(BF16)
        terms = [dst.at[part].reshape(halo, 128)[...] for part in range(parts)]
        total = mm(chosen[:, :halo], terms[0])
        for part in range(1, parts):
            total = total + mm(chosen[:, part * halo : part * halo + halo], terms[part])
        snap_send[which] = total
        snap_recv[which, mine] = total
        for k in range(1, n_snap):
            pltpu.make_async_remote_copy(
                snap_send.at[which], snap_recv.at[which, mine], snap_s.at[which], snap_r.at[which],
                device_id={"snap": (mine + k) % n_snap}, device_id_type=MESH,
            ).start()

    def finish_pieces(group, which, piece):
        others = snap_recv.at[which, pl.ds(0, n_snap - 1)]
        pltpu.make_async_copy(others, others, snap_r.at[which]).wait()
        total = snap_recv[which, 0]
        for k in range(1, n_snap):
            total = total + snap_recv[which, k]
        slots = piece.shape[1]
        for part in range(piece.shape[0]):
            piece[part] = total[part * slots : (part + 1) * slots, :].astype(BF16)
        spread_piece(group, piece)

    def gathered(group, tile, count):
        at = tile * count
        return recv_buf(group).at[at // halo].reshape(halo, 128)[at % halo : at % halo + count, :]

    def far(hop):
        dst = recv_buf(hop)
        span = 256 if hop < 2 else 128
        got = [dst.at[part].reshape(halo, 128)[...] for part in range(span // 128)]
        got = got[0] if len(got) == 1 else jnp.concatenate(got, axis=1)
        both = mm(sw[...], got)
        low = lanes(width, span) % 128 < 64
        return jnp.where(low, both[:width, :], both[width:, :])

    start = jnp.concatenate([held[...], extra], axis=1)
    launch(0, start.astype(BF16))

    wts = [columns[:, 8 + d : 9 + d] for d in range(degs)]
    srcs = [columns[:, d : d + 1].astype(jnp.int32) for d in range(degs)]
    for first in range(0, width, 128):
        here = lanes(128, width + halo)
        total = jnp.zeros((128, width + halo), F32)
        for d in range(degs):
            total = total + jnp.where(srcs[d][first : first + 128] == here, wts[d][first : first + 128], 0.0)
        total = total.astype(BF16)
        wl[first : first + 128, :] = total[:, :width]
        sw[width + first : width + first + 128, :] = total[:, width:]
    deg_near = []
    for first in range(0, width, 128):
        block = push_block(first, 128)
        ml[first : first + 128, :] = block.astype(BF16)
        deg_near.append(jnp.sum(block, axis=1, keepdims=True))
    deg_near = jnp.concatenate(deg_near, axis=0)
    sw[:width, :] = jnp.where(
        lax.broadcasted_iota(jnp.int32, (width, halo), 0) == sr_ref[...], 1.0, 0.0
    ).astype(BF16)
    deg_in = wts[0]
    for d in range(1, degs):
        deg_in = deg_in + wts[d]
    inv_in = 1.0 / deg_in

    cols = gw_ref.shape[0]
    pick[...] = jnp.where(
        lax.broadcasted_iota(jnp.int32, (cols, 512), 0) == forward_map(lanes(1, 512), chans, fin), 1.0, 0.0
    ).astype(BF16)
    column = lax.broadcasted_iota(jnp.int32, (512, 1), 0)
    back_pick[...] = jnp.where(lanes(512, cols) == forward_map(column, chans, fin), 1.0, 0.0).astype(BF16)
    adjoint_pick = jnp.where(
        lanes(384, cols) == backward_map(column[:384], chans, fin), 1.0, 0.0
    ).astype(BF16)
    gate_w = gw_ref[...]
    cand_w = cw_ref[...]
    gate_f = mm(back_pick[...], gate_w)
    turned = pltpu.roll(gate_f, 64, 1)
    low512 = lanes(512, 128) < 64
    wg[:, :128] = jnp.where(low512, gate_f, turned).astype(BF16)
    wg[:, 128:] = jnp.where(low512, turned, gate_f).astype(BF16)
    wc[...] = mm_t1(back_pick[...], jnp.concatenate([cand_w, cand_w], axis=0)).astype(BF16)
    bg[...] = jnp.transpose(mm(adjoint_pick, gate_w)).astype(BF16)
    bc[:64, :] = mm_t1(cand_w, adjoint_pick).astype(BF16)
    bc[64:, :] = jnp.zeros((64, 384), BF16)
    bias2[0:1, :64] = cb_ref[...]
    bias2[0:1, 64:] = cb_ref[...]

    wide[...] = near(start.astype(BF16))
    await_recv(0)
    raw = far(0)
    deg_out = deg_near + raw[:, 128 + fin : 129 + fin] + raw[:, 129 + fin : 130 + fin]
    raw = raw + wide[...]
    inv_out = 1.0 / deg_out
    scale_f[...] = jnp.where(low128, inv_out, inv_in)
    scale_a[...] = jnp.where(low128, inv_in, inv_out)
    first_main = (raw[:, :128] * scale_f[...]).astype(BF16)
    states[:, :128] = first_main
    first_extra = jnp.where(lane128 % 64 < fin, raw[:, 128:] * scale_f[...], 0.0)
    second_in = jnp.concatenate([first_main, first_extra.astype(BF16)], axis=1)
    launch(1, second_in)
    ones = jnp.where(
        low128, held[...], jnp.where(lane128 < 64 + fin, extra, jnp.where(lane128 == 64 + fin, 1.0, 0.0))
    )
    states[:, 256:384] = ones.astype(BF16)
    wide[...] = near(second_in)
    await_recv(1)
    raw = far(1) + wide[...]
    states[:, 128:256] = (2.0 * raw[:, :128] * scale_f[...] - held[...]).astype(BF16)
    second_extra = 2.0 * raw[:, 128:] * scale_f[...] - extra
    tail = first_extra.astype(BF16).astype(F32) + pltpu.roll(second_extra.astype(BF16).astype(F32), fin, 1)
    states[:, 384:] = tail.astype(BF16)

    gates = mm(states[...], wg[...])
    bias = jnp.broadcast_to(gb_ref[...], (width, 128))
    turned = pltpu.roll(bias, 64, 1)
    reset = jax.nn.sigmoid(gates[:, :128] + jnp.where(low128, bias, turned))
    update = jax.nn.sigmoid(gates[:, 128:] + jnp.where(low128, turned, bias))
    scaled = (reset * held[...]).astype(BF16)

    launch(2, scaled)
    mixed[:, 256:384] = jnp.where(low128, scaled, states[:, 256:384])
    mixed[:, 384:] = states[:, 384:]
    local[...] = near(scaled)
    await_recv(2)
    hop_one = ((far(2) + local[...]) * scale_f[...]).astype(BF16)
    launch(3, hop_one)
    mixed[:, :128] = hop_one
    local[...] = near(hop_one)
    await_recv(3)
    raw = far(3) + local[...]
    mixed[:, 128:256] = (2.0 * raw * scale_f[...] - scaled.astype(F32)).astype(BF16)
    cand = jnp.tanh(mm(mixed[...], wc[...]) + bias2[0:1, :])
    cand_grad = (upward[...] * (1.0 - update) * (1.0 - cand * cand)).astype(BF16)

    update_part = upward[...] * (held[...] - cand) * update * (1.0 - update)

    def outer_hop(grad, weights, hop):
        outer = mm(grad, weights[:, :128])
        values = (outer * scale_a[...]).astype(BF16)
        launch(hop, values)
        return outer, values

    def inner_hop(grad, weights, hop, outer, values, meanwhile):
        local[...] = near(values)
        inner = mm(grad, weights[:, 128:256])
        field[...] = mm(grad, weights[:, 256:384]) - outer - pltpu.roll(outer, 64, 1)
        meanwhile()
        await_recv(hop)
        raw = far(hop) + local[...]
        values = ((inner + 2.0 * raw) * scale_a[...]).astype(BF16)
        launch(hop + 1, values)
        local[...] = near(values)

    def last_hop(hop):
        await_recv(hop)
        raw = far(hop) + local[...]
        return field[...] + raw + pltpu.roll(raw, 64, 1)

    def early_sums():
        grads = turn(jnp.where(low128, cand_grad.astype(F32), update_part)).astype(BF16)
        by_cand = mm(grads[:64, :], mixed[...])
        by_update = mm(grads[64:, :], states[...])
        for tile in range(4):
            dst = early.at[0, tile // 2].reshape(halo, 128)
            at = tile % 2 * 128
            dst[at : at + 64, :] = by_cand[:, tile * 128 : tile * 128 + 128].astype(BF16)
            dst[at + 64 : at + 128, :] = by_update[:, tile * 128 : tile * 128 + 128].astype(BF16)
        send_all(RS_EARLY)

    outer, values = outer_hop(cand_grad, bc, 4)
    inner_hop(cand_grad, bc, 4, outer, values, early_sums)
    reduce_pieces(RS_EARLY, 0)
    scaled_grad = last_hop(5)
    reset_part = scaled_grad * held[...] * reset * (1.0 - reset)
    gate_grad = jnp.where(low128, reset_part, update_part).astype(BF16)
    outer, values = outer_hop(gate_grad, bg, 6)
    by_reset = mm(turn(gate_grad)[:64, :].astype(BF16), states[...])
    for tile in range(4):
        late.at[0, 0].reshape(halo, 128)[tile * 64 : tile * 64 + 64, :] = by_reset[
            :, tile * 128 : tile * 128 + 128
        ].astype(BF16)
    send_all(RS_LATE)
    inner_hop(gate_grad, bg, 6, outer, values, lambda: finish_pieces(AG_EARLY, 0, piece_e))
    reduce_pieces(RS_LATE, 1)
    finish_pieces(AG_LATE, 1, piece_l)

    await_recv(AG_EARLY)
    bias_row = jnp.where(lanes(8, 128) == 64 + fin, 1.0, 0.0).astype(BF16)

    def put_bias(tiles, bias_out):
        bias_out[...] = mm_t1(bias_row, tiles[2])[0:1, :] * factor

    tiles = [gathered(AG_EARLY, tile, 128)[:64] for tile in range(4)]
    total = mm(tiles[0], back_pick[:128, :])
    for tile in range(1, 4):
        total = total + mm(tiles[tile], back_pick[tile * 128 : tile * 128 + 128, :])
    cand_out[...] = total * factor
    put_bias(tiles, cand_bias_out)
    state_part = last_hop(7)
    result = upward[...] * update + scaled_grad * reset + state_part
    state_ref[0] = jnp.transpose(result)[:64, :].astype(BF16)
    await_recv(AG_LATE)
    tiles = [
        jnp.concatenate([gathered(AG_LATE, tile, 64), gathered(AG_EARLY, tile, 128)[64:]], axis=0)
        for tile in range(4)
    ]
    total = mm_t1(pick[:, :128], tiles[0])
    for tile in range(1, 4):
        total = total + mm_t1(pick[:, tile * 128 : tile * 128 + 128], tiles[tile])
    gate_out[...] = total * factor
    put_bias(tiles, gate_bias_out)

    for group in range(GROUPS):
        rest = recv_buf(group).at[:, pl.ds(0, n_dom - 1)]
        pltpu.make_async_copy(rest, rest, ssem.at[group]).wait()
    for which in range(2):
        others = snap_recv.at[which, pl.ds(0, n_snap - 1)]
        pltpu.make_async_copy(others, others, snap_s.at[which]).wait()


def solution(mesh):
    n_dom, n_snap = mesh.shape["dom"], mesh.shape["snap"]

    def body(readings, previous, upstream, gw, gb, cw, cb, nb, ew, sr):
        fin, hidden, width = readings.shape[1], previous.shape[1], readings.shape[2]
        chans, halo = fin + hidden, sr.shape[1]
        slots = halo // n_dom
        vmem = pl.BlockSpec(memory_space=pltpu.VMEM)

        factor = 1.0 / math.sqrt(readings.shape[0] * n_snap * width * n_dom)

        def run(*refs):
            kernel(n_dom, n_snap, width, fin, chans, halo, factor, *refs)

        cols = gw.shape[1]
        arrays = (readings, previous, upstream, gw.T, gb.reshape(1, -1), cw, cb.reshape(1, -1), nb, ew, sr)
        state, gate, gate_b, cand, cand_b = pl.pallas_call(
            run,
            out_shape=(
                jax.ShapeDtypeStruct((1, hidden, width), BF16),
                jax.ShapeDtypeStruct((cols, 2 * hidden), F32),
                jax.ShapeDtypeStruct((1, 2 * hidden), F32),
                jax.ShapeDtypeStruct((hidden, cols), F32),
                jax.ShapeDtypeStruct((1, hidden), F32),
            ),
            in_specs=[pl.BlockSpec(memory_space=pl.ANY)] * 10,
            out_specs=(vmem,) * 5,
            scratch_shapes=[
                pltpu.VMEM((2 * halo, width), BF16),
                pltpu.VMEM((width, width), BF16),
                pltpu.VMEM((width, width), BF16),
                pltpu.VMEM((2 * width, halo), BF16),
                pltpu.VMEM((width, 128), F32),
                pltpu.VMEM((width, 128), F32),
                pltpu.VMEM((width, 128), F32),
                pltpu.VMEM((width, 128), F32),
                pltpu.VMEM((width, 128), F32),
                pltpu.VMEM((width, 256), F32),
                pltpu.VMEM((width, 512), BF16),
                pltpu.VMEM((width, 512), BF16),
                pltpu.VMEM((width, 128), F32),
                pltpu.VMEM((512, 256), BF16),
                pltpu.VMEM((512, 128), BF16),
                pltpu.VMEM((128, 384), BF16),
                pltpu.VMEM((128, 384), BF16),
                pltpu.VMEM((2, 2, n_dom, slots, 128), BF16),
                pltpu.VMEM((2, 2, n_dom, slots, 128), BF16),
                pltpu.VMEM((HOPS - 2, 1, n_dom, slots, 128), BF16),
                pltpu.VMEM((HOPS - 2, 1, n_dom, slots, 128), BF16),
                pltpu.SemaphoreType.DMA((GROUPS,)),
                pltpu.SemaphoreType.DMA((GROUPS,)),
                pltpu.SemaphoreType.DMA((GROUPS,)),
                pltpu.VMEM((2, 128, width), F32),
                pltpu.VMEM((3, 2, n_dom, slots, 128), BF16),
                pltpu.VMEM((3, 1, n_dom, slots, 128), BF16),
                pltpu.VMEM((2, slots, 128), BF16),
                pltpu.VMEM((1, slots, 128), BF16),
                pltpu.VMEM((2, 8, 128), F32),
                pltpu.VMEM((2, n_snap, 8, 128), F32),
                pltpu.SemaphoreType.DMA((2,)),
                pltpu.SemaphoreType.DMA((2,)),
                pltpu.VMEM((512, cols), BF16),
                pltpu.VMEM((cols, 512), BF16),
                pltpu.VMEM((8, 128), F32),
                *(pltpu.VMEM(array.shape, array.dtype) for array in arrays),
                pltpu.SemaphoreType.DMA((len(arrays),)),
            ],
            compiler_params=pltpu.CompilerParams(collective_id=0, has_side_effects=True),
        )(*arrays)
        return state, gate.T, gate_b.reshape(-1), cand, cand_b.reshape(-1)

    in_specs = (
        P("snap", None, "dom"), P("snap", None, "dom"), P("snap", None, "dom"),
        P(), P(), P(), P(), P(None, "dom"), P(None, "dom"), P("dom", None),
    )
    out_specs = (P("snap", None, "dom"), P(), P(), P(), P())
    return jax.shard_map(body, mesh=mesh, in_specs=in_specs, out_specs=out_specs, check_vma=False)
```

```python
import math

import jax
import jax.numpy as jnp
from jax import lax
from jax.experimental import pallas as pl
from jax.experimental.pallas import tpu as pltpu
from jax.sharding import PartitionSpec as P

F32, BF16 = jnp.float32, jnp.bfloat16
MESH = pl.DeviceIdType.MESH
HOPS = 8
RS_EARLY, AG_EARLY, RS_LATE, AG_LATE, GROUPS = 8, 9, 10, 11, 12
NY, NZ, NC = 4, 8, 2


def mm(a, b):
    return jnp.dot(a, b, preferred_element_type=F32)


def mm_t1(a, b):
    return lax.dot_general(a, b, (((1,), (1,)), ((), ())), preferred_element_type=F32)


def turn(a):
    return jnp.transpose(a.astype(F32))


def lanes(rows, width):
    return lax.broadcasted_iota(jnp.int32, (rows, width), 1)


def forward_map(lane, chans, fin):
    tile, at = lane // 128, lane % 128
    upper, low = at >= 64, at % 64
    first = jnp.where(upper, 3 * chans, chans) + fin + low
    second = jnp.where(upper, 4 * chans, 2 * chans) + fin + low
    third = jnp.where(upper, jnp.where(low < fin, low, -1), fin + low)
    order = jnp.where(upper, 3, 1) + low // fin
    fourth = jnp.where(low < 2 * fin, order * chans + low % fin, -1)
    return jnp.where(tile == 0, first, jnp.where(tile == 1, second, jnp.where(tile == 2, third, fourth)))


def backward_map(lane, chans, fin):
    tile, at = lane // 128, lane % 128
    upper, low = at >= 64, at % 64
    order = jnp.where(
        tile == 0, jnp.where(upper, 2, 4), jnp.where(tile == 1, jnp.where(upper, 1, 3), 0)
    )
    return order * chans + fin + low


def kernel(
    n_dom, n_snap, width, fin, chans, halo, factor,
    *refs,
):
    sources, refs = refs[:10], refs[10:]
    landed, refs = refs[-11:-1], refs[:-11] + refs[-1:]
    copies = [
        pltpu.make_async_copy(src, dst, refs[-1].at[at]) for at, (src, dst) in enumerate(zip(sources, landed))
    ]
    for copy in copies:
        copy.start()
    step(n_dom, n_snap, width, fin, chans, halo, factor, copies, *landed, *refs[:-1])


def step(
    n_dom, n_snap, width, fin, chans, halo, factor, copies,
    readings_ref, previous_ref, upstream_ref, gw_ref, gb_ref, cw_ref, cb_ref, nb_ref, ew_ref, sr_ref,
    state_ref, gate_out, gate_bias_out, cand_out, cand_bias_out,
    sp, near_m, far_m, held, upward, scale_f, scale_a, local, wide, states, mixed, field, wg, wc, bg, bc,
    send_w, recv_w, send_n, recv_n, ssem, rsem, osem, rows,
    early, late, piece_e, piece_l, snap_send, snap_recv, snap_s, snap_r, back_pick, pick, bias2,
    gate_r, gate_u, slope_c, slope_r, part, inner_v,
):
    me = lax.axis_index("dom")
    barrier = pltpu.get_barrier_semaphore()

    my_core, my_z, my_y = me % NC, me // NC % NZ, me // (NC * NZ)

    def each_peer(visit):
        def ring(t, c):
            z = (my_z + NZ + NZ // 2 + (t + 1) // 2 * (1 - t % 2 * 2)) % NZ
            for dy in (2, 1, 3, 0):
                for dc in range(NC):
                    visit(((my_y + dy) % NY * NZ + z) * NC + (my_core + dc) % NC)
            return c

        lax.fori_loop(0, NZ - 1, ring, 0)
        for dy in (2, 1, 3, 0):
            for dc in range(NC):
                if dy or dc:
                    visit(((my_y + dy) % NY * NZ + my_z) * NC + (my_core + dc) % NC)

    each_peer(lambda peer: pl.semaphore_signal(barrier, inc=1, device_id={"dom": peer}, device_id_type=MESH))
    mine = lax.axis_index("snap")
    for k in range(1, n_snap):
        pl.semaphore_signal(barrier, inc=1, device_id={"snap": (mine + k) % n_snap}, device_id_type=MESH)

    for copy in copies:
        copy.wait()
    lane128 = lanes(width, 128)
    low128 = lane128 < 64

    prev = previous_ref[0].astype(F32)
    held[...] = jnp.transpose(jnp.concatenate([prev, prev], axis=0))
    ups = upstream_ref[0].astype(F32)
    upward[...] = jnp.transpose(jnp.concatenate([ups, ups], axis=0))
    read = readings_ref[0].astype(F32)
    degs = nb_ref.shape[0]
    rows[...] = jnp.zeros_like(rows)
    rows[0, 0:fin, :] = read
    rows[0, 64 : 64 + fin, :] = read
    rows[1, 0:degs, :] = nb_ref[...].astype(F32)
    rows[1, 8 : 8 + degs, :] = ew_ref[...]
    rows[1, 16:17, :halo] = sr_ref[...].astype(F32)
    extra = jnp.transpose(rows[0])
    columns = jnp.transpose(rows[1])

    rows_sel = columns[:halo, 16:17].astype(jnp.int32)
    sp[:, width:] = jnp.where(lanes(halo, width) == rows_sel, 1.0, 0.0).astype(BF16)

    def push_block(first, rows):
        here = lax.broadcasted_iota(jnp.int32, (rows, width), 0) + first
        total = jnp.zeros((rows, width), F32)
        for d in range(degs):
            total = total + jnp.where(nb_ref[d : d + 1, :] == here, ew_ref[d : d + 1, :], 0.0)
        return total

    edge_sums = push_block(width, halo)
    sp[:, :width] = edge_sums.astype(BF16)
    deg_halo = jnp.sum(edge_sums, axis=1, keepdims=True)
    deg_high = deg_halo.astype(BF16).astype(F32)
    deg_rest = deg_halo - deg_high

    def send_buf(hop):
        if hop >= HOPS:
            return {RS_EARLY: early.at[0], RS_LATE: late.at[0]}[hop]
        return send_w.at[hop] if hop < 2 else send_n.at[hop - 2]

    def recv_buf(hop):
        if hop >= HOPS:
            return {RS_EARLY: early.at[1], AG_EARLY: early.at[2], RS_LATE: late.at[1], AG_LATE: late.at[2]}[hop]
        return recv_w.at[hop] if hop < 2 else recv_n.at[hop - 2]

    def send_all(group):
        src, dst = send_buf(group), recv_buf(group)

        def go(peer):
            pltpu.make_async_remote_copy(
                src.at[:, peer], dst.at[:, me], ssem.at[group], rsem.at[group],
                device_id={"dom": peer}, device_id_type=MESH,
            ).start()

        each_peer(go)
        pltpu.make_async_copy(src.at[:, me], dst.at[:, me], osem.at[group]).start()

    def spread_piece(group, src):
        dst = recv_buf(group)

        def go(peer):
            pltpu.make_async_remote_copy(
                src, dst.at[:, me], ssem.at[group], rsem.at[group],
                device_id={"dom": peer}, device_id_type=MESH,
            ).start()

        each_peer(go)
        pltpu.make_async_copy(src, dst.at[:, me], osem.at[group]).start()

    def halves(values):
        low = jnp.where(lanes(*values.shape) % 128 < 64, 1.0, 0.0).astype(BF16)
        return jnp.concatenate([values * low, values * (1.0 - low)], axis=0)

    def launch(hop, values):
        span = values.shape[1]
        out = mm(sp[...], halves(values))
        if hop == 0:
            lane = lanes(halo, span)
            out = jnp.where(lane == 128 + fin, deg_high, jnp.where(lane == 128 + fin + 1, deg_rest, out))
        out = out.astype(BF16)
        src = send_buf(hop)
        for part in range(span // 128):
            src.at[part].reshape(halo, 128)[...] = out[:, part * 128 : part * 128 + 128]

        if hop == 0:
            pl.semaphore_wait(barrier, n_dom + n_snap - 2)
        send_all(hop)

    def near(values):
        return mm(near_m[...], halves(values))

    def await_recv(hop):
        dst = recv_buf(hop)
        rest = dst.at[:, pl.ds(0, n_dom - 1)]
        pltpu.make_async_copy(rest, rest, rsem.at[hop]).wait()
        pltpu.make_async_copy(dst.at[:, me], dst.at[:, me], osem.at[hop]).wait()

    def reduce_pieces(group, which):
        await_recv(group)
        dst = recv_buf(group)
        parts = dst.shape[0]
        row = lax.broadcasted_iota(jnp.int32, (8, halo * parts), 0)
        col = lanes(8, halo * parts)
        slots = dst.shape[2]
        chosen = (col % slots == row % slots) & (col // halo == (row // slots) % parts)
        chosen = jnp.where(chosen, 1.0, 0.0).astype(BF16)
        terms = [dst.at[part].reshape(halo, 128)[...] for part in range(parts)]
        total = mm(chosen[:, :halo], terms[0])
        for part in range(1, parts):
            total = total + mm(chosen[:, part * halo : part * halo + halo], terms[part])
        snap_send[which] = total
        snap_recv[which, mine] = total
        for k in range(1, n_snap):
            pltpu.make_async_remote_copy(
                snap_send.at[which], snap_recv.at[which, mine], snap_s.at[which], snap_r.at[which],
                device_id={"snap": (mine + k) % n_snap}, device_id_type=MESH,
            ).start()

    def finish_pieces(group, which, piece):
        others = snap_recv.at[which, pl.ds(0, n_snap - 1)]
        pltpu.make_async_copy(others, others, snap_r.at[which]).wait()
        total = snap_recv[which, 0]
        for k in range(1, n_snap):
            total = total + snap_recv[which, k]
        slots = piece.shape[1]
        for part in range(piece.shape[0]):
            piece[part] = total[part * slots : (part + 1) * slots, :].astype(BF16)
        spread_piece(group, piece)

    def gathered(group, tile, count):
        at = tile * count
        return recv_buf(group).at[at // halo].reshape(halo, 128)[at % halo : at % halo + count, :]

    def far(hop):
        dst = recv_buf(hop)
        got = [dst.at[part].reshape(halo, 128)[...] for part in range(dst.shape[0])]
        got = got[0] if len(got) == 1 else jnp.concatenate(got, axis=1)
        return mm(far_m[...], halves(got))

    start = jnp.concatenate([held[...], extra], axis=1)
    launch(0, start.astype(BF16))

    wts = [columns[:, 8 + d : 9 + d] for d in range(degs)]
    srcs = [columns[:, d : d + 1].astype(jnp.int32) for d in range(degs)]
    for first in range(0, width, 128):
        here = lanes(128, width + halo)
        total = jnp.zeros((128, width + halo), F32)
        for d in range(degs):
            total = total + jnp.where(srcs[d][first : first + 128] == here, wts[d][first : first + 128], 0.0)
        total = total.astype(BF16)
        near_m[first : first + 128, width:] = total[:, :width]
        far_m[first : first + 128, halo:] = total[:, width:]
    deg_near = []
    for first in range(0, width, 128):
        block = push_block(first, 128)
        near_m[first : first + 128, :width] = block.astype(BF16)
        deg_near.append(jnp.sum(block, axis=1, keepdims=True))
    deg_near = jnp.concatenate(deg_near, axis=0)
    far_m[:, :halo] = jnp.where(
        lax.broadcasted_iota(jnp.int32, (width, halo), 0) == sr_ref[...], 1.0, 0.0
    ).astype(BF16)
    deg_in = wts[0]
    for d in range(1, degs):
        deg_in = deg_in + wts[d]
    inv_in = 1.0 / deg_in

    cols = gw_ref.shape[0]
    pick[...] = jnp.where(
        lax.broadcasted_iota(jnp.int32, (cols, 512), 0) == forward_map(lanes(1, 512), chans, fin), 1.0, 0.0
    ).astype(BF16)
    column = lax.broadcasted_iota(jnp.int32, (512, 1), 0)
    back_pick[...] = jnp.where(lanes(512, cols) == forward_map(column, chans, fin), 1.0, 0.0).astype(BF16)
    adjoint_pick = jnp.where(
        lanes(384, cols) == backward_map(column[:384], chans, fin), 1.0, 0.0
    ).astype(BF16)
    gate_w = gw_ref[...]
    cand_w = cw_ref[...]
    gate_f = mm(back_pick[...], gate_w)
    turned = pltpu.roll(gate_f, 64, 1)
    low512 = lanes(512, 128) < 64
    wg[:, :128] = jnp.where(low512, gate_f, turned).astype(BF16)
    wg[:, 128:] = jnp.where(low512, turned, gate_f).astype(BF16)
    wc[...] = mm_t1(back_pick[...], jnp.concatenate([cand_w, cand_w], axis=0)).astype(BF16)
    bg[...] = jnp.transpose(mm(adjoint_pick, gate_w)).astype(BF16)
    bc[:64, :] = mm_t1(cand_w, adjoint_pick).astype(BF16)
    bc[64:, :] = jnp.zeros((64, 384), BF16)
    bias2[0:1, :64] = cb_ref[...]
    bias2[0:1, 64:] = cb_ref[...]

    wide[...] = near(start.astype(BF16))
    await_recv(0)
    raw = far(0)
    deg_out = deg_near + raw[:, 128 + fin : 129 + fin] + raw[:, 129 + fin : 130 + fin]
    raw = raw + wide[...]
    inv_out = 1.0 / deg_out
    scale_f[...] = jnp.where(low128, inv_out, inv_in)
    scale_a[...] = jnp.where(low128, inv_in, inv_out)
    first_main = (raw[:, :128] * scale_f[...]).astype(BF16)
    states[:, :128] = first_main
    first_extra = jnp.where(lane128 % 64 < fin, raw[:, 128:] * scale_f[...], 0.0)
    second_in = jnp.concatenate([first_main, first_extra.astype(BF16)], axis=1)
    launch(1, second_in)
    ones = jnp.where(
        low128, held[...], jnp.where(lane128 < 64 + fin, extra, jnp.where(lane128 == 64 + fin, 1.0, 0.0))
    )
    states[:, 256:384] = ones.astype(BF16)
    wide[...] = near(second_in)
    bias = jnp.broadcast_to(gb_ref[...], (width, 128))
    turned = pltpu.roll(bias, 64, 1)
    local[...] = (
        mm(states[:, :128], wg[:128, :128])
        + mm(states[:, 256:384], wg[256:384, :128])
        + jnp.where(low128, bias, turned)
    )
    await_recv(1)
    raw = far(1) + wide[...]
    states[:, 128:256] = (2.0 * raw[:, :128] * scale_f[...] - held[...]).astype(BF16)
    second_extra = 2.0 * raw[:, 128:] * scale_f[...] - extra
    tail = first_extra.astype(BF16).astype(F32) + pltpu.roll(second_extra.astype(BF16).astype(F32), fin, 1)
    states[:, 384:] = tail.astype(BF16)

    reset = jax.nn.sigmoid(
        local[...] + mm(states[:, 128:256], wg[128:256, :128]) + mm(states[:, 384:], wg[384:, :128])
    )
    scaled = (reset * held[...]).astype(BF16)
    launch(2, scaled)
    local[...] = near(scaled)
    update = jax.nn.sigmoid(mm(states[...], wg[:, 128:]) + jnp.where(low128, turned, bias))
    gate_r[...] = reset
    gate_u[...] = update
    slope_c[...] = upward[...] * (1.0 - update)
    slope_r[...] = held[...] * reset * (1.0 - reset)
    mixed[:, 256:384] = jnp.where(low128, scaled, states[:, 256:384])
    mixed[:, 384:] = states[:, 384:]
    await_recv(2)
    hop_one = ((far(2) + local[...]) * scale_f[...]).astype(BF16)
    launch(3, hop_one)
    mixed[:, :128] = hop_one
    local[...] = near(hop_one)
    part[...] = (
        mm(mixed[:, :128], wc[:128, :]) + mm(mixed[:, 256:], wc[256:, :]) + bias2[0:1, :]
    )
    await_recv(3)
    raw = far(3) + local[...]
    mixed[:, 128:256] = (2.0 * raw * scale_f[...] - scaled.astype(F32)).astype(BF16)
    cand = jnp.tanh(part[...] + mm(mixed[:, 128:256], wc[128:256, :]))
    cand_grad = (slope_c[...] * (1.0 - cand * cand)).astype(BF16)

    def outer_hop(grad, weights, hop):
        outer = mm(grad, weights[:, :128])
        values = (outer * scale_a[...]).astype(BF16)
        launch(hop, values)
        return outer, values

    def inner_hop(grad, weights, hop, outer, values, meanwhile):
        local[...] = near(values)
        inner_v[...] = mm(grad, weights[:, 128:256])
        field[...] = mm(grad, weights[:, 256:384]) - outer - pltpu.roll(outer, 64, 1)
        meanwhile()
        await_recv(hop)
        raw = far(hop) + local[...]
        values = ((inner_v[...] + 2.0 * raw) * scale_a[...]).astype(BF16)
        launch(hop + 1, values)
        local[...] = near(values)

    def last_hop(hop):
        await_recv(hop)
        raw = far(hop) + local[...]
        return field[...] + raw + pltpu.roll(raw, 64, 1)

    def early_sums():
        update_part = upward[...] * (held[...] - cand) * gate_u[...] * (1.0 - gate_u[...])
        part[...] = update_part
        grads = turn(jnp.where(low128, cand_grad.astype(F32), update_part)).astype(BF16)
        by_cand = mm(grads[:64, :], mixed[...])
        by_update = mm(grads[64:, :], states[...])
        for tile in range(4):
            dst = early.at[0, tile // 2].reshape(halo, 128)
            at = tile % 2 * 128
            dst[at : at + 64, :] = by_cand[:, tile * 128 : tile * 128 + 128].astype(BF16)
            dst[at + 64 : at + 128, :] = by_update[:, tile * 128 : tile * 128 + 128].astype(BF16)
        send_all(RS_EARLY)

    outer, values = outer_hop(cand_grad, bc, 4)
    inner_hop(cand_grad, bc, 4, outer, values, early_sums)
    reduce_pieces(RS_EARLY, 0)
    finish_pieces(AG_EARLY, 0, piece_e)
    scaled_grad = last_hop(5)
    gate_grad = jnp.where(low128, scaled_grad * slope_r[...], part[...]).astype(BF16)
    by_reset = mm(turn(gate_grad)[:64, :].astype(BF16), states[...])
    for tile in range(4):
        late.at[0, 0].reshape(halo, 128)[tile * 64 : tile * 64 + 64, :] = by_reset[
            :, tile * 128 : tile * 128 + 128
        ].astype(BF16)
    send_all(RS_LATE)
    outer, values = outer_hop(gate_grad, bg, 6)
    part[...] = upward[...] * gate_u[...] + scaled_grad * gate_r[...]
    inner_hop(gate_grad, bg, 6, outer, values, lambda: reduce_pieces(RS_LATE, 1))
    field[...] = field[...] + part[...]
    finish_pieces(AG_LATE, 1, piece_l)

    await_recv(AG_EARLY)
    bias_row = jnp.where(lanes(8, 128) == 64 + fin, 1.0, 0.0).astype(BF16)

    def put_bias(tiles, bias_out):
        bias_out[...] = mm_t1(bias_row, tiles[2])[0:1, :] * factor

    tiles = [gathered(AG_EARLY, tile, 128)[:64] for tile in range(4)]
    total = mm(tiles[0], back_pick[:128, :])
    for tile in range(1, 4):
        total = total + mm(tiles[tile], back_pick[tile * 128 : tile * 128 + 128, :])
    cand_out[...] = total * factor
    put_bias(tiles, cand_bias_out)
    state_ref[0] = jnp.transpose(last_hop(7))[:64, :].astype(BF16)
    await_recv(AG_LATE)
    tiles = [
        jnp.concatenate([gathered(AG_LATE, tile, 64), gathered(AG_EARLY, tile, 128)[64:]], axis=0)
        for tile in range(4)
    ]
    total = mm_t1(pick[:, :128], tiles[0])
    for tile in range(1, 4):
        total = total + mm_t1(pick[:, tile * 128 : tile * 128 + 128], tiles[tile])
    gate_out[...] = total * factor
    put_bias(tiles, gate_bias_out)

    for group in range(GROUPS):
        rest = recv_buf(group).at[:, pl.ds(0, n_dom - 1)]
        pltpu.make_async_copy(rest, rest, ssem.at[group]).wait()
    for which in range(2):
        others = snap_recv.at[which, pl.ds(0, n_snap - 1)]
        pltpu.make_async_copy(others, others, snap_s.at[which]).wait()


def solution(mesh):
    n_dom, n_snap = mesh.shape["dom"], mesh.shape["snap"]

    def body(readings, previous, upstream, gw, gb, cw, cb, nb, ew, sr):
        fin, hidden, width = readings.shape[1], previous.shape[1], readings.shape[2]
        chans, halo = fin + hidden, sr.shape[1]
        slots = halo // n_dom
        vmem = pl.BlockSpec(memory_space=pltpu.VMEM)

        factor = 1.0 / math.sqrt(readings.shape[0] * n_snap * width * n_dom)

        def run(*refs):
            kernel(n_dom, n_snap, width, fin, chans, halo, factor, *refs)

        cols = gw.shape[1]
        arrays = (readings, previous, upstream, gw.T, gb.reshape(1, -1), cw, cb.reshape(1, -1), nb, ew, sr)
        state, gate, gate_b, cand, cand_b = pl.pallas_call(
            run,
            out_shape=(
                jax.ShapeDtypeStruct((1, hidden, width), BF16),
                jax.ShapeDtypeStruct((cols, 2 * hidden), F32),
                jax.ShapeDtypeStruct((1, 2 * hidden), F32),
                jax.ShapeDtypeStruct((hidden, cols), F32),
                jax.ShapeDtypeStruct((1, hidden), F32),
            ),
            in_specs=[pl.BlockSpec(memory_space=pl.ANY)] * 10,
            out_specs=(vmem,) * 5,
            scratch_shapes=[
                pltpu.VMEM((halo, 2 * width), BF16),
                pltpu.VMEM((width, 2 * width), BF16),
                pltpu.VMEM((width, 2 * halo), BF16),
                pltpu.VMEM((width, 128), F32),
                pltpu.VMEM((width, 128), F32),
                pltpu.VMEM((width, 128), F32),
                pltpu.VMEM((width, 128), F32),
                pltpu.VMEM((width, 128), F32),
                pltpu.VMEM((width, 256), F32),
                pltpu.VMEM((width, 512), BF16),
                pltpu.VMEM((width, 512), BF16),
                pltpu.VMEM((width, 128), F32),
                pltpu.VMEM((512, 256), BF16),
                pltpu.VMEM((512, 128), BF16),
                pltpu.VMEM((128, 384), BF16),
                pltpu.VMEM((128, 384), BF16),
                pltpu.VMEM((2, 2, n_dom, slots, 128), BF16),
                pltpu.VMEM((2, 2, n_dom, slots, 128), BF16),
                pltpu.VMEM((HOPS - 2, 1, n_dom, slots, 128), BF16),
                pltpu.VMEM((HOPS - 2, 1, n_dom, slots, 128), BF16),
                pltpu.SemaphoreType.DMA((GROUPS,)),
                pltpu.SemaphoreType.DMA((GROUPS,)),
                pltpu.SemaphoreType.DMA((GROUPS,)),
                pltpu.VMEM((2, 128, width), F32),
                pltpu.VMEM((3, 2, n_dom, slots, 128), BF16),
                pltpu.VMEM((3, 1, n_dom, slots, 128), BF16),
                pltpu.VMEM((2, slots, 128), BF16),
                pltpu.VMEM((1, slots, 128), BF16),
                pltpu.VMEM((2, 8, 128), F32),
                pltpu.VMEM((2, n_snap, 8, 128), F32),
                pltpu.SemaphoreType.DMA((2,)),
                pltpu.SemaphoreType.DMA((2,)),
                pltpu.VMEM((512, cols), BF16),
                pltpu.VMEM((cols, 512), BF16),
                pltpu.VMEM((8, 128), F32),
                *[pltpu.VMEM((width, 128), F32)] * 6,
                *(pltpu.VMEM(array.shape, array.dtype) for array in arrays),
                pltpu.SemaphoreType.DMA((len(arrays),)),
            ],
            compiler_params=pltpu.CompilerParams(collective_id=0, has_side_effects=True),
        )(*arrays)
        results = (state, gate, gate_b, cand, cand_b)

        def write(*refs):
            for src, dst in zip(refs[: len(results)], refs[len(results) :]):
                dst[...] = src[...]

        state, gate, gate_b, cand, cand_b = pl.pallas_call(
            write,
            out_shape=tuple(jax.ShapeDtypeStruct(array.shape, array.dtype) for array in results),
            in_specs=[vmem] * len(results),
            out_specs=(vmem,) * len(results),
        )(*results)
        return state, gate.T, gate_b.reshape(-1), cand, cand_b.reshape(-1)

    in_specs = (
        P("snap", None, "dom"), P("snap", None, "dom"), P("snap", None, "dom"),
        P(), P(), P(), P(), P(None, "dom"), P(None, "dom"), P("dom", None),
    )
    out_specs = (P("snap", None, "dom"), P(), P(), P(), P())
    return jax.shard_map(body, mesh=mesh, in_specs=in_specs, out_specs=out_specs, check_vma=False)
```

```python
import math

import jax
import jax.numpy as jnp
from jax import lax
from jax.experimental import pallas as pl
from jax.experimental.pallas import tpu as pltpu
from jax.sharding import PartitionSpec as P

F32, BF16 = jnp.float32, jnp.bfloat16
MESH = pl.DeviceIdType.MESH
HOPS = 8
RS_EARLY, AG_EARLY, RS_LATE, AG_LATE, GROUPS = 8, 9, 10, 11, 12
NY, NZ, NC = 4, 8, 2


def mm(a, b):
    return jnp.dot(a, b, preferred_element_type=F32)


def mm_t1(a, b):
    return lax.dot_general(a, b, (((1,), (1,)), ((), ())), preferred_element_type=F32)


def turn(a):
    return jnp.transpose(a.astype(F32))


def lanes(rows, width):
    return lax.broadcasted_iota(jnp.int32, (rows, width), 1)


def forward_map(lane, chans, fin):
    tile, at = lane // 128, lane % 128
    upper, low = at >= 64, at % 64
    first = jnp.where(upper, 3 * chans, chans) + fin + low
    second = jnp.where(upper, 4 * chans, 2 * chans) + fin + low
    third = jnp.where(upper, jnp.where(low < fin, low, -1), fin + low)
    order = jnp.where(upper, 3, 1) + low // fin
    fourth = jnp.where(low < 2 * fin, order * chans + low % fin, -1)
    return jnp.where(tile == 0, first, jnp.where(tile == 1, second, jnp.where(tile == 2, third, fourth)))


def backward_map(lane, chans, fin):
    tile, at = lane // 128, lane % 128
    upper, low = at >= 64, at % 64
    order = jnp.where(
        tile == 0, jnp.where(upper, 2, 4), jnp.where(tile == 1, jnp.where(upper, 1, 3), 0)
    )
    return order * chans + fin + low


def kernel(
    n_dom, n_snap, width, fin, chans, halo, factor,
    *refs,
):
    sources, refs = refs[:10], refs[10:]
    landed, refs = refs[-11:-1], refs[:-11] + refs[-1:]
    copies = [
        pltpu.make_async_copy(src, dst, refs[-1].at[at]) for at, (src, dst) in enumerate(zip(sources, landed))
    ]
    for copy in copies:
        copy.start()
    step(n_dom, n_snap, width, fin, chans, halo, factor, copies, *landed, *refs[:-1])


def step(
    n_dom, n_snap, width, fin, chans, halo, factor, copies,
    readings_ref, previous_ref, upstream_ref, gw_ref, gb_ref, cw_ref, cb_ref, nb_ref, ew_ref, sr_ref,
    state_ref, gate_out, gate_bias_out, cand_out, cand_bias_out,
    sp, ml, wl, sw, comp_f, comp_a, held, upward, scale_f, scale_a, local, wide, states, mixed, field, wg, wc, bg, bc,
    send_w, recv_w, send_n, recv_n, ssem, rsem, osem, rows,
    early, late, piece_e, piece_l, snap_send, snap_recv, snap_s, snap_r, back_pick, pick, bias2,
    gate_r, gate_u, slope_c, slope_r, part, inner_v, ahead,
):
    me = lax.axis_index("dom")
    barrier = pltpu.get_barrier_semaphore()

    my_core, my_z, my_y = me % NC, me // NC % NZ, me // (NC * NZ)

    def each_peer(visit):
        def ring(t, c):
            z = (my_z + NZ + NZ // 2 + (t + 1) // 2 * (1 - t % 2 * 2)) % NZ
            for dy in (2, 1, 3, 0):
                for dc in range(NC):
                    visit(((my_y + dy) % NY * NZ + z) * NC + (my_core + dc) % NC)
            return c

        lax.fori_loop(0, NZ - 1, ring, 0)
        for dy in (2, 1, 3, 0):
            for dc in range(NC):
                if dy or dc:
                    visit(((my_y + dy) % NY * NZ + my_z) * NC + (my_core + dc) % NC)

    each_peer(lambda peer: pl.semaphore_signal(barrier, inc=1, device_id={"dom": peer}, device_id_type=MESH))
    mine = lax.axis_index("snap")
    for k in range(1, n_snap):
        pl.semaphore_signal(barrier, inc=1, device_id={"snap": (mine + k) % n_snap}, device_id_type=MESH)

    for copy in copies:
        copy.wait()
    lane128 = lanes(width, 128)
    low128 = lane128 < 64

    prev = previous_ref[0].astype(F32)
    held[...] = jnp.transpose(jnp.concatenate([prev, prev], axis=0))
    ups = upstream_ref[0].astype(F32)
    upward[...] = jnp.transpose(jnp.concatenate([ups, ups], axis=0))
    read = readings_ref[0].astype(F32)
    degs = nb_ref.shape[0]
    rows[...] = jnp.zeros_like(rows)
    rows[0, 0:fin, :] = read
    rows[0, 64 : 64 + fin, :] = read
    rows[1, 0:degs, :] = nb_ref[...].astype(F32)
    rows[1, 8 : 8 + degs, :] = ew_ref[...]
    rows[1, 16:17, :halo] = sr_ref[...].astype(F32)
    extra = jnp.transpose(rows[0])
    columns = jnp.transpose(rows[1])

    rows_sel = columns[:halo, 16:17].astype(jnp.int32)
    sp[:halo, :] = jnp.where(lanes(halo, width) == rows_sel, 1.0, 0.0).astype(BF16)

    def push_block(first, rows):
        here = lax.broadcasted_iota(jnp.int32, (rows, width), 0) + first
        total = jnp.zeros((rows, width), F32)
        for d in range(degs):
            total = total + jnp.where(nb_ref[d : d + 1, :] == here, ew_ref[d : d + 1, :], 0.0)
        return total

    edge_sums = push_block(width, halo)
    sp[halo:, :] = edge_sums.astype(BF16)
    deg_halo = jnp.sum(edge_sums, axis=1, keepdims=True)
    deg_high = deg_halo.astype(BF16).astype(F32)
    deg_rest = deg_halo - deg_high

    def send_buf(hop):
        if hop >= HOPS:
            return {RS_EARLY: early.at[0], RS_LATE: late.at[0]}[hop]
        return send_w.at[hop] if hop < 2 else send_n.at[hop - 2]

    def recv_buf(hop):
        if hop >= HOPS:
            return {RS_EARLY: early.at[1], AG_EARLY: early.at[2], RS_LATE: late.at[1], AG_LATE: late.at[2]}[hop]
        return recv_w.at[hop] if hop < 2 else recv_n.at[hop - 2]

    def send_all(group):
        src, dst = send_buf(group), recv_buf(group)

        def go(peer):
            pltpu.make_async_remote_copy(
                src.at[:, peer], dst.at[:, me], ssem.at[group], rsem.at[group],
                device_id={"dom": peer}, device_id_type=MESH,
            ).start()

        each_peer(go)
        pltpu.make_async_copy(src.at[:, me], dst.at[:, me], osem.at[group]).start()

    def spread_piece(group, src):
        dst = recv_buf(group)

        def go(peer):
            pltpu.make_async_remote_copy(
                src, dst.at[:, me], ssem.at[group], rsem.at[group],
                device_id={"dom": peer}, device_id_type=MESH,
            ).start()

        each_peer(go)
        pltpu.make_async_copy(src, dst.at[:, me], osem.at[group]).start()

    def to_send(values):
        rows = mm(sp[...], values)
        return jnp.where(lanes(halo, values.shape[1]) % 128 < 64, rows[halo:, :], rows[:halo, :])

    def launch(hop, out):
        span = out.shape[1]
        if hop == 0:
            lane = lanes(halo, span)
            out = jnp.where(lane == 128 + fin, deg_high, jnp.where(lane == 128 + fin + 1, deg_rest, out))
        out = out.astype(BF16)
        src = send_buf(hop)
        for part in range(span // 128):
            src.at[part].reshape(halo, 128)[...] = out[:, part * 128 : part * 128 + 128]

        if hop == 0:
            pl.semaphore_wait(barrier, n_dom + n_snap - 2)
        send_all(hop)

    def near(values):
        low = lanes(*values.shape) % 128 < 64
        return jnp.where(low, mm(ml[...], values), mm(wl[...], values))

    def await_recv(hop):
        dst = recv_buf(hop)
        rest = dst.at[:, pl.ds(0, n_dom - 1)]
        pltpu.make_async_copy(rest, rest, rsem.at[hop]).wait()
        pltpu.make_async_copy(dst.at[:, me], dst.at[:, me], osem.at[hop]).wait()

    def reduce_pieces(group, which):
        await_recv(group)
        dst = recv_buf(group)
        parts = dst.shape[0]
        row = lax.broadcasted_iota(jnp.int32, (8, halo * parts), 0)
        col = lanes(8, halo * parts)
        slots = dst.shape[2]
        chosen = (col % slots == row % slots) & (col // halo == (row // slots) % parts)
        chosen = jnp.where(chosen, 1.0, 0.0).astype(BF16)
        terms = [dst.at[part].reshape(halo, 128)[...] for part in range(parts)]
        total = mm(chosen[:, :halo], terms[0])
        for part in range(1, parts):
            total = total + mm(chosen[:, part * halo : part * halo + halo], terms[part])
        snap_send[which] = total
        snap_recv[which, mine] = total
        for k in range(1, n_snap):
            pltpu.make_async_remote_copy(
                snap_send.at[which], snap_recv.at[which, mine], snap_s.at[which], snap_r.at[which],
                device_id={"snap": (mine + k) % n_snap}, device_id_type=MESH,
            ).start()

    def finish_pieces(group, which, piece):
        others = snap_recv.at[which, pl.ds(0, n_snap - 1)]
        pltpu.make_async_copy(others, others, snap_r.at[which]).wait()
        total = snap_recv[which, 0]
        for k in range(1, n_snap):
            total = total + snap_recv[which, k]
        slots = piece.shape[1]
        for part in range(piece.shape[0]):
            piece[part] = total[part * slots : (part + 1) * slots, :].astype(BF16)
        spread_piece(group, piece)

    def gathered(group, tile, count):
        at = tile * count
        return recv_buf(group).at[at // halo].reshape(halo, 128)[at % halo : at % halo + count, :]

    def arrived(hop):
        dst = recv_buf(hop)
        got = [dst.at[part].reshape(halo, 128)[...] for part in range(dst.shape[0])]
        return got[0] if len(got) == 1 else jnp.concatenate(got, axis=1)

    def far(got):
        both = mm(sw[...], got)
        low = lanes(width, got.shape[1]) % 128 < 64
        return jnp.where(low, both[:width, :], both[width:, :])

    def onward(got, composed):
        rows = mm(composed[...], got)
        return jnp.where(lanes(halo, 128) < 64, rows[halo:, :], rows[:halo, :])

    start = jnp.concatenate([held[...], extra], axis=1)
    launch(0, to_send(start.astype(BF16)))

    wts = [columns[:, 8 + d : 9 + d] for d in range(degs)]
    srcs = [columns[:, d : d + 1].astype(jnp.int32) for d in range(degs)]
    for first in range(0, width, 128):
        here = lanes(128, width + halo)
        total = jnp.zeros((128, width + halo), F32)
        for d in range(degs):
            total = total + jnp.where(srcs[d][first : first + 128] == here, wts[d][first : first + 128], 0.0)
        total = total.astype(BF16)
        wl[first : first + 128, :] = total[:, :width]
        sw[width + first : width + first + 128, :] = total[:, width:]
    deg_near = []
    for first in range(0, width, 128):
        block = push_block(first, 128)
        ml[first : first + 128, :] = block.astype(BF16)
        deg_near.append(jnp.sum(block, axis=1, keepdims=True))
    deg_near = jnp.concatenate(deg_near, axis=0)
    sw[:width, :] = jnp.where(
        lax.broadcasted_iota(jnp.int32, (width, halo), 0) == sr_ref[...], 1.0, 0.0
    ).astype(BF16)
    deg_in = wts[0]
    for d in range(1, degs):
        deg_in = deg_in + wts[d]
    inv_in = 1.0 / deg_in

    cols = gw_ref.shape[0]
    pick[...] = jnp.where(
        lax.broadcasted_iota(jnp.int32, (cols, 512), 0) == forward_map(lanes(1, 512), chans, fin), 1.0, 0.0
    ).astype(BF16)
    column = lax.broadcasted_iota(jnp.int32, (512, 1), 0)
    back_pick[...] = jnp.where(lanes(512, cols) == forward_map(column, chans, fin), 1.0, 0.0).astype(BF16)
    adjoint_pick = jnp.where(
        lanes(384, cols) == backward_map(column[:384], chans, fin), 1.0, 0.0
    ).astype(BF16)
    gate_w = gw_ref[...]
    cand_w = cw_ref[...]
    gate_f = mm(back_pick[...], gate_w)
    turned = pltpu.roll(gate_f, 64, 1)
    low512 = lanes(512, 128) < 64
    wg[:, :128] = jnp.where(low512, gate_f, turned).astype(BF16)
    wg[:, 128:] = jnp.where(low512, turned, gate_f).astype(BF16)
    wc[...] = mm_t1(back_pick[...], jnp.concatenate([cand_w, cand_w], axis=0)).astype(BF16)
    bg[...] = jnp.transpose(mm(adjoint_pick, gate_w)).astype(BF16)
    bc[:64, :] = mm_t1(cand_w, adjoint_pick).astype(BF16)
    bc[64:, :] = jnp.zeros((64, 384), BF16)
    bias2[0:1, :64] = cb_ref[...]
    bias2[0:1, 64:] = cb_ref[...]

    wide[...] = near(start.astype(BF16))
    await_recv(0)
    raw = far(arrived(0))
    deg_out = deg_near + raw[:, 128 + fin : 129 + fin] + raw[:, 129 + fin : 130 + fin]
    raw = raw + wide[...]
    inv_out = 1.0 / deg_out
    scale_f[...] = jnp.where(low128, inv_out, inv_in)
    scale_a[...] = jnp.where(low128, inv_in, inv_out)
    first_main = (raw[:, :128] * scale_f[...]).astype(BF16)
    states[:, :128] = first_main
    first_extra = jnp.where(lane128 % 64 < fin, raw[:, 128:] * scale_f[...], 0.0)
    second_in = jnp.concatenate([first_main, first_extra.astype(BF16)], axis=1)
    launch(1, to_send(second_in))
    for comp, times, by_push, by_pull in ((comp_f, 1.0, inv_out, inv_in), (comp_a, 2.0, inv_in, inv_out)):
        pushed = (sw[:width, :].astype(F32) * by_push).astype(BF16)
        pulled = (sw[width:, :].astype(F32) * by_pull).astype(BF16)
        comp[halo:, :] = (mm(sp[halo:, :], pushed) * times).astype(BF16)
        comp[:halo, :] = (mm(sp[:halo, :], pulled) * times).astype(BF16)
    ones = jnp.where(
        low128, held[...], jnp.where(lane128 < 64 + fin, extra, jnp.where(lane128 == 64 + fin, 1.0, 0.0))
    )
    states[:, 256:384] = ones.astype(BF16)
    wide[...] = near(second_in)
    bias = jnp.broadcast_to(gb_ref[...], (width, 128))
    turned = pltpu.roll(bias, 64, 1)
    local[...] = (
        mm(states[:, :128], wg[:128, :128])
        + mm(states[:, 256:384], wg[256:384, :128])
        + jnp.where(low128, bias, turned)
    )
    await_recv(1)
    raw = far(arrived(1)) + wide[...]
    states[:, 128:256] = (2.0 * raw[:, :128] * scale_f[...] - held[...]).astype(BF16)
    second_extra = 2.0 * raw[:, 128:] * scale_f[...] - extra
    tail = first_extra.astype(BF16).astype(F32) + pltpu.roll(second_extra.astype(BF16).astype(F32), fin, 1)
    states[:, 384:] = tail.astype(BF16)

    reset = jax.nn.sigmoid(
        local[...] + mm(states[:, 128:256], wg[128:256, :128]) + mm(states[:, 384:], wg[384:, :128])
    )
    scaled = (reset * held[...]).astype(BF16)
    launch(2, to_send(scaled))
    beside = near(scaled)
    local[...] = beside
    ahead[...] = to_send((beside * scale_f[...]).astype(BF16))
    update = jax.nn.sigmoid(mm(states[...], wg[:, 128:]) + jnp.where(low128, turned, bias))
    gate_r[...] = reset
    gate_u[...] = update
    slope_c[...] = upward[...] * (1.0 - update)
    slope_r[...] = held[...] * reset * (1.0 - reset)
    mixed[:, 256:384] = jnp.where(low128, scaled, states[:, 256:384])
    mixed[:, 384:] = states[:, 384:]
    await_recv(2)
    got = arrived(2)
    launch(3, ahead[...] + onward(got, comp_f))
    hop_one = ((far(got) + local[...]) * scale_f[...]).astype(BF16)
    mixed[:, :128] = hop_one
    local[...] = near(hop_one)
    part[...] = (
        mm(mixed[:, :128], wc[:128, :]) + mm(mixed[:, 256:], wc[256:, :]) + bias2[0:1, :]
    )
    await_recv(3)
    raw = far(arrived(3)) + local[...]
    mixed[:, 128:256] = (2.0 * raw * scale_f[...] - scaled.astype(F32)).astype(BF16)
    cand = jnp.tanh(part[...] + mm(mixed[:, 128:256], wc[128:256, :]))
    cand_grad = (slope_c[...] * (1.0 - cand * cand)).astype(BF16)

    def outer_hop(grad, weights, hop):
        outer = mm(grad, weights[:, :128])
        values = (outer * scale_a[...]).astype(BF16)
        launch(hop, to_send(values))
        return outer, values

    def inner_hop(grad, weights, hop, outer, values, meanwhile):
        beside = near(values)
        local[...] = beside
        inner = mm(grad, weights[:, 128:256])
        inner_v[...] = inner
        ahead[...] = to_send(((inner + 2.0 * beside) * scale_a[...]).astype(BF16))
        field[...] = mm(grad, weights[:, 256:384]) - outer - pltpu.roll(outer, 64, 1)
        meanwhile()
        await_recv(hop)
        got = arrived(hop)
        launch(hop + 1, ahead[...] + onward(got, comp_a))
        raw = far(got) + local[...]
        values = ((inner_v[...] + 2.0 * raw) * scale_a[...]).astype(BF16)
        local[...] = near(values)

    def last_hop(hop):
        await_recv(hop)
        raw = far(arrived(hop)) + local[...]
        return field[...] + raw + pltpu.roll(raw, 64, 1)

    def early_sums():
        update_part = upward[...] * (held[...] - cand) * gate_u[...] * (1.0 - gate_u[...])
        part[...] = update_part
        grads = turn(jnp.where(low128, cand_grad.astype(F32), update_part)).astype(BF16)
        by_cand = mm(grads[:64, :], mixed[...])
        by_update = mm(grads[64:, :], states[...])
        for tile in range(4):
            dst = early.at[0, tile // 2].reshape(halo, 128)
            at = tile % 2 * 128
            dst[at : at + 64, :] = by_cand[:, tile * 128 : tile * 128 + 128].astype(BF16)
            dst[at + 64 : at + 128, :] = by_update[:, tile * 128 : tile * 128 + 128].astype(BF16)
        send_all(RS_EARLY)

    outer, values = outer_hop(cand_grad, bc, 4)
    inner_hop(cand_grad, bc, 4, outer, values, early_sums)
    reduce_pieces(RS_EARLY, 0)
    scaled_grad = last_hop(5)
    gate_grad = jnp.where(low128, scaled_grad * slope_r[...], part[...]).astype(BF16)
    by_reset = mm(turn(gate_grad)[:64, :].astype(BF16), states[...])
    for tile in range(4):
        late.at[0, 0].reshape(halo, 128)[tile * 64 : tile * 64 + 64, :] = by_reset[
            :, tile * 128 : tile * 128 + 128
        ].astype(BF16)
    send_all(RS_LATE)
    outer, values = outer_hop(gate_grad, bg, 6)
    finish_pieces(AG_EARLY, 0, piece_e)
    part[...] = upward[...] * gate_u[...] + scaled_grad * gate_r[...]
    inner_hop(gate_grad, bg, 6, outer, values, lambda: reduce_pieces(RS_LATE, 1))
    field[...] = field[...] + part[...]
    finish_pieces(AG_LATE, 1, piece_l)

    await_recv(AG_EARLY)
    bias_row = jnp.where(lanes(8, 128) == 64 + fin, 1.0, 0.0).astype(BF16)

    def put_bias(tiles, bias_out):
        bias_out[...] = mm_t1(bias_row, tiles[2])[0:1, :] * factor

    tiles = [gathered(AG_EARLY, tile, 128)[:64] for tile in range(4)]
    total = mm(tiles[0], back_pick[:128, :])
    for tile in range(1, 4):
        total = total + mm(tiles[tile], back_pick[tile * 128 : tile * 128 + 128, :])
    cand_out[...] = total * factor
    put_bias(tiles, cand_bias_out)
    state_ref[0] = jnp.transpose(last_hop(7))[:64, :].astype(BF16)
    await_recv(AG_LATE)
    tiles = [
        jnp.concatenate([gathered(AG_LATE, tile, 64), gathered(AG_EARLY, tile, 128)[64:]], axis=0)
        for tile in range(4)
    ]
    total = mm_t1(pick[:, :128], tiles[0])
    for tile in range(1, 4):
        total = total + mm_t1(pick[:, tile * 128 : tile * 128 + 128], tiles[tile])
    gate_out[...] = total * factor
    put_bias(tiles, gate_bias_out)

    for group in range(GROUPS):
        rest = recv_buf(group).at[:, pl.ds(0, n_dom - 1)]
        pltpu.make_async_copy(rest, rest, ssem.at[group]).wait()
    for which in range(2):
        others = snap_recv.at[which, pl.ds(0, n_snap - 1)]
        pltpu.make_async_copy(others, others, snap_s.at[which]).wait()


def solution(mesh):
    n_dom, n_snap = mesh.shape["dom"], mesh.shape["snap"]

    def body(readings, previous, upstream, gw, gb, cw, cb, nb, ew, sr):
        fin, hidden, width = readings.shape[1], previous.shape[1], readings.shape[2]
        chans, halo = fin + hidden, sr.shape[1]
        slots = halo // n_dom
        vmem = pl.BlockSpec(memory_space=pltpu.VMEM)

        factor = 1.0 / math.sqrt(readings.shape[0] * n_snap * width * n_dom)

        def run(*refs):
            kernel(n_dom, n_snap, width, fin, chans, halo, factor, *refs)

        cols = gw.shape[1]
        arrays = (readings, previous, upstream, gw.T, gb.reshape(1, -1), cw, cb.reshape(1, -1), nb, ew, sr)
        state, gate, gate_b, cand, cand_b = pl.pallas_call(
            run,
            out_shape=(
                jax.ShapeDtypeStruct((1, hidden, width), BF16),
                jax.ShapeDtypeStruct((cols, 2 * hidden), F32),
                jax.ShapeDtypeStruct((1, 2 * hidden), F32),
                jax.ShapeDtypeStruct((hidden, cols), F32),
                jax.ShapeDtypeStruct((1, hidden), F32),
            ),
            in_specs=[pl.BlockSpec(memory_space=pl.ANY)] * 10,
            out_specs=(vmem,) * 5,
            scratch_shapes=[
                pltpu.VMEM((2 * halo, width), BF16),
                pltpu.VMEM((width, width), BF16),
                pltpu.VMEM((width, width), BF16),
                pltpu.VMEM((2 * width, halo), BF16),
                pltpu.VMEM((2 * halo, halo), BF16),
                pltpu.VMEM((2 * halo, halo), BF16),
                pltpu.VMEM((width, 128), F32),
                pltpu.VMEM((width, 128), F32),
                pltpu.VMEM((width, 128), F32),
                pltpu.VMEM((width, 128), F32),
                pltpu.VMEM((width, 128), F32),
                pltpu.VMEM((width, 256), F32),
                pltpu.VMEM((width, 512), BF16),
                pltpu.VMEM((width, 512), BF16),
                pltpu.VMEM((width, 128), F32),
                pltpu.VMEM((512, 256), BF16),
                pltpu.VMEM((512, 128), BF16),
                pltpu.VMEM((128, 384), BF16),
                pltpu.VMEM((128, 384), BF16),
                pltpu.VMEM((2, 2, n_dom, slots, 128), BF16),
                pltpu.VMEM((2, 2, n_dom, slots, 128), BF16),
                pltpu.VMEM((HOPS - 2, 1, n_dom, slots, 128), BF16),
                pltpu.VMEM((HOPS - 2, 1, n_dom, slots, 128), BF16),
                pltpu.SemaphoreType.DMA((GROUPS,)),
                pltpu.SemaphoreType.DMA((GROUPS,)),
                pltpu.SemaphoreType.DMA((GROUPS,)),
                pltpu.VMEM((2, 128, width), F32),
                pltpu.VMEM((3, 2, n_dom, slots, 128), BF16),
                pltpu.VMEM((3, 1, n_dom, slots, 128), BF16),
                pltpu.VMEM((2, slots, 128), BF16),
                pltpu.VMEM((1, slots, 128), BF16),
                pltpu.VMEM((2, 8, 128), F32),
                pltpu.VMEM((2, n_snap, 8, 128), F32),
                pltpu.SemaphoreType.DMA((2,)),
                pltpu.SemaphoreType.DMA((2,)),
                pltpu.VMEM((512, cols), BF16),
                pltpu.VMEM((cols, 512), BF16),
                pltpu.VMEM((8, 128), F32),
                *[pltpu.VMEM((width, 128), F32)] * 6,
                pltpu.VMEM((halo, 128), F32),
                *(pltpu.VMEM(array.shape, array.dtype) for array in arrays),
                pltpu.SemaphoreType.DMA((len(arrays),)),
            ],
            compiler_params=pltpu.CompilerParams(collective_id=0, has_side_effects=True),
        )(*arrays)
        results = (state, gate, gate_b, cand, cand_b)

        def write(*refs):
            for src, dst in zip(refs[: len(results)], refs[len(results) :]):
                dst[...] = src[...]

        state, gate, gate_b, cand, cand_b = pl.pallas_call(
            write,
            out_shape=tuple(jax.ShapeDtypeStruct(array.shape, array.dtype) for array in results),
            in_specs=[vmem] * len(results),
            out_specs=(vmem,) * len(results),
        )(*results)
        return state, gate.T, gate_b.reshape(-1), cand, cand_b.reshape(-1)

    in_specs = (
        P("snap", None, "dom"), P("snap", None, "dom"), P("snap", None, "dom"),
        P(), P(), P(), P(), P(None, "dom"), P(None, "dom"), P("dom", None),
    )
    out_specs = (P("snap", None, "dom"), P(), P(), P(), P())
    return jax.shard_map(body, mesh=mesh, in_specs=in_specs, out_specs=out_specs, check_vma=False)
```

```python
import math

import jax
import jax.numpy as jnp
from jax import lax
from jax.experimental import pallas as pl
from jax.experimental.pallas import tpu as pltpu
from jax.sharding import PartitionSpec as P

F32, BF16 = jnp.float32, jnp.bfloat16
MESH = pl.DeviceIdType.MESH
HOPS = 8
RS_EARLY, AG_EARLY, RS_LATE, AG_LATE, GROUPS = 8, 9, 10, 11, 12
NY, NZ, NC = 4, 8, 2


def mm(a, b):
    return jnp.dot(a, b, preferred_element_type=F32)


def mm_t1(a, b):
    return lax.dot_general(a, b, (((1,), (1,)), ((), ())), preferred_element_type=F32)


def turn(a):
    return jnp.transpose(a.astype(F32))


def lanes(rows, width):
    return lax.broadcasted_iota(jnp.int32, (rows, width), 1)


def forward_map(lane, chans, fin):
    tile, at = lane // 128, lane % 128
    upper, low = at >= 64, at % 64
    first = jnp.where(upper, 3 * chans, chans) + fin + low
    second = jnp.where(upper, 4 * chans, 2 * chans) + fin + low
    third = jnp.where(upper, jnp.where(low < fin, low, -1), fin + low)
    order = jnp.where(upper, 3, 1) + low // fin
    fourth = jnp.where(low < 2 * fin, order * chans + low % fin, -1)
    return jnp.where(tile == 0, first, jnp.where(tile == 1, second, jnp.where(tile == 2, third, fourth)))


def backward_map(lane, chans, fin):
    tile, at = lane // 128, lane % 128
    upper, low = at >= 64, at % 64
    order = jnp.where(
        tile == 0, jnp.where(upper, 2, 4), jnp.where(tile == 1, jnp.where(upper, 1, 3), 0)
    )
    return order * chans + fin + low


def kernel(
    n_dom, n_snap, width, fin, chans, halo, factor,
    *refs,
):
    sources, refs = refs[:10], refs[10:]
    landed, refs = refs[-11:-1], refs[:-11] + refs[-1:]
    copies = [
        pltpu.make_async_copy(src, dst, refs[-1].at[at]) for at, (src, dst) in enumerate(zip(sources, landed))
    ]
    for copy in copies:
        copy.start()
    step(n_dom, n_snap, width, fin, chans, halo, factor, copies, *landed, *refs[:-1])


def step(
    n_dom, n_snap, width, fin, chans, halo, factor, copies,
    readings_ref, previous_ref, upstream_ref, gw_ref, gb_ref, cw_ref, cb_ref, nb_ref, ew_ref, sr_ref,
    state_ref, gate_out, gate_bias_out, cand_out, cand_bias_out,
    sp, ml, wl, sw, comp_f, comp_a, held, upward, scale_f, scale_a, local, wide, states, mixed, field, wg, wc, bg, bc,
    send_w, recv_w, send_n, recv_n, ssem, rsem, osem, rows,
    early, late, piece_e, piece_l, snap_send, snap_recv, snap_s, snap_r, back_pick, pick, bias2,
    gate_r, gate_u, slope_c, slope_r, part, inner_v, ahead, z_send, z_recv,
):
    me = lax.axis_index("dom")
    barrier = pltpu.get_barrier_semaphore()

    my_core, my_z, my_y = me % NC, me // NC % NZ, me // (NC * NZ)

    def each_peer(visit):
        def ring(t, c):
            z = (my_z + NZ + NZ // 2 + (t + 1) // 2 * (1 - t % 2 * 2)) % NZ
            for dy in (2, 1, 3, 0):
                for dc in range(NC):
                    visit(((my_y + dy) % NY * NZ + z) * NC + (my_core + dc) % NC)
            return c

        lax.fori_loop(0, NZ - 1, ring, 0)
        for dy in (2, 1, 3, 0):
            for dc in range(NC):
                if dy or dc:
                    visit(((my_y + dy) % NY * NZ + my_z) * NC + (my_core + dc) % NC)

    each_peer(lambda peer: pl.semaphore_signal(barrier, inc=1, device_id={"dom": peer}, device_id_type=MESH))
    mine = lax.axis_index("snap")
    plane = n_snap * NY * NC
    my_place = (mine * NY + my_y) * NC + my_core

    def each_mate(visit):
        for dx in (2, 1, 3, 0):
            for dy in (2, 1, 3, 0):
                for dc in range(NC):
                    if dx or dy or dc:
                        x, y, c = (mine + dx) % n_snap, (my_y + dy) % NY, (my_core + dc) % NC
                        visit((x * NY + y) * NC + c, {"snap": x, "dom": (y * NZ + my_z) * NC + c})

    for dx in range(1, n_snap):
        for dy in range(NY):
            for dc in range(NC):
                x, y, c = (mine + dx) % n_snap, (my_y + dy) % NY, (my_core + dc) % NC
                pl.semaphore_signal(
                    barrier, inc=1, device_id={"snap": x, "dom": (y * NZ + my_z) * NC + c}, device_id_type=MESH
                )

    for copy in copies:
        copy.wait()
    lane128 = lanes(width, 128)
    low128 = lane128 < 64

    prev = previous_ref[0].astype(F32)
    held[...] = jnp.transpose(jnp.concatenate([prev, prev], axis=0))
    ups = upstream_ref[0].astype(F32)
    upward[...] = jnp.transpose(jnp.concatenate([ups, ups], axis=0))
    read = readings_ref[0].astype(F32)
    degs = nb_ref.shape[0]
    rows[...] = jnp.zeros_like(rows)
    rows[0, 0:fin, :] = read
    rows[0, 64 : 64 + fin, :] = read
    rows[1, 0:degs, :] = nb_ref[...].astype(F32)
    rows[1, 8 : 8 + degs, :] = ew_ref[...]
    rows[1, 16:17, :halo] = sr_ref[...].astype(F32)
    extra = jnp.transpose(rows[0])
    columns = jnp.transpose(rows[1])

    rows_sel = columns[:halo, 16:17].astype(jnp.int32)
    sp[:halo, :] = jnp.where(lanes(halo, width) == rows_sel, 1.0, 0.0).astype(BF16)

    def push_block(first, rows):
        here = lax.broadcasted_iota(jnp.int32, (rows, width), 0) + first
        total = jnp.zeros((rows, width), F32)
        for d in range(degs):
            total = total + jnp.where(nb_ref[d : d + 1, :] == here, ew_ref[d : d + 1, :], 0.0)
        return total

    edge_sums = push_block(width, halo)
    sp[halo:, :] = edge_sums.astype(BF16)
    deg_halo = jnp.sum(edge_sums, axis=1, keepdims=True)
    deg_high = deg_halo.astype(BF16).astype(F32)
    deg_rest = deg_halo - deg_high

    def send_buf(hop):
        if hop >= HOPS:
            return early.at[0]
        return send_w.at[hop] if hop < 2 else send_n.at[hop - 2]

    def recv_buf(hop):
        if hop >= HOPS:
            return early.at[1] if hop == RS_EARLY else early.at[2]
        return recv_w.at[hop] if hop < 2 else recv_n.at[hop - 2]

    def send_all(group):
        src, dst = send_buf(group), recv_buf(group)

        def go(peer):
            pltpu.make_async_remote_copy(
                src.at[:, peer], dst.at[:, me], ssem.at[group], rsem.at[group],
                device_id={"dom": peer}, device_id_type=MESH,
            ).start()

        each_peer(go)
        pltpu.make_async_copy(src.at[:, me], dst.at[:, me], osem.at[group]).start()

    def spread_piece(group, src):
        dst = recv_buf(group)

        def go(peer):
            pltpu.make_async_remote_copy(
                src, dst.at[:, me], ssem.at[group], rsem.at[group],
                device_id={"dom": peer}, device_id_type=MESH,
            ).start()

        each_peer(go)
        pltpu.make_async_copy(src, dst.at[:, me], osem.at[group]).start()

    def to_send(values):
        rows = mm(sp[...], values)
        return jnp.where(lanes(halo, values.shape[1]) % 128 < 64, rows[halo:, :], rows[:halo, :])

    def launch(hop, out):
        span = out.shape[1]
        if hop == 0:
            lane = lanes(halo, span)
            out = jnp.where(lane == 128 + fin, deg_high, jnp.where(lane == 128 + fin + 1, deg_rest, out))
        out = out.astype(BF16)
        src = send_buf(hop)
        for part in range(span // 128):
            src.at[part].reshape(halo, 128)[...] = out[:, part * 128 : part * 128 + 128]

        if hop == 0:
            pl.semaphore_wait(barrier, n_dom - 1 + (n_snap - 1) * NY * NC)
        send_all(hop)

    def near(values):
        low = lanes(*values.shape) % 128 < 64
        return jnp.where(low, mm(ml[...], values), mm(wl[...], values))

    def await_recv(hop):
        dst = recv_buf(hop)
        rest = dst.at[:, pl.ds(0, n_dom - 1)]
        pltpu.make_async_copy(rest, rest, rsem.at[hop]).wait()
        pltpu.make_async_copy(dst.at[:, me], dst.at[:, me], osem.at[hop]).wait()

    def reduce_pieces(group, which):
        await_recv(group)
        dst = recv_buf(group)
        parts = dst.shape[0]
        row = lax.broadcasted_iota(jnp.int32, (8, halo * parts), 0)
        col = lanes(8, halo * parts)
        slots = dst.shape[2]
        chosen = (col % slots == row % slots) & (col // halo == (row // slots) % parts)
        chosen = jnp.where(chosen, 1.0, 0.0).astype(BF16)
        terms = [dst.at[part].reshape(halo, 128)[...] for part in range(parts)]
        total = mm(chosen[:, :halo], terms[0])
        for part in range(1, parts):
            total = total + mm(chosen[:, part * halo : part * halo + halo], terms[part])
        snap_send[which] = total
        snap_recv[which, mine] = total
        for k in range(1, n_snap):
            pltpu.make_async_remote_copy(
                snap_send.at[which], snap_recv.at[which, mine], snap_s.at[which], snap_r.at[which],
                device_id={"snap": (mine + k) % n_snap}, device_id_type=MESH,
            ).start()

    def finish_pieces(group, which, piece):
        others = snap_recv.at[which, pl.ds(0, n_snap - 1)]
        pltpu.make_async_copy(others, others, snap_r.at[which]).wait()
        total = snap_recv[which, 0]
        for k in range(1, n_snap):
            total = total + snap_recv[which, k]
        slots = piece.shape[1]
        for part in range(piece.shape[0]):
            piece[part] = total[part * slots : (part + 1) * slots, :].astype(BF16)
        spread_piece(group, piece)

    def gathered(tile):
        at = tile * 128
        return early.at[2, at // halo].reshape(halo, 128)[at % halo : at % halo + 128, :]

    def late_send(group, piece_of):
        dst = late.at[1] if group == RS_LATE else late.at[2]

        def go(place, device):
            pltpu.make_async_remote_copy(
                piece_of(place), dst.at[my_place], ssem.at[group], rsem.at[group],
                device_id=device, device_id_type=MESH,
            ).start()

        each_mate(go)
        pltpu.make_async_copy(piece_of(my_place), dst.at[my_place], osem.at[group]).start()

    def late_await(group):
        dst = late.at[1] if group == RS_LATE else late.at[2]
        rest = dst.at[pl.ds(0, plane - 1)]
        pltpu.make_async_copy(rest, rest, rsem.at[group]).wait()
        pltpu.make_async_copy(dst.at[my_place], dst.at[my_place], osem.at[group]).wait()

    def z_copies():
        for dz in (4, 3, 5, 2, 6, 1, 7):
            yield pltpu.make_async_remote_copy(
                z_send, z_recv.at[my_z], snap_s.at[1], snap_r.at[1],
                device_id={"dom": (my_y * NZ + (my_z + dz) % NZ) * NC + my_core}, device_id_type=MESH,
            )

    def late_reduce():
        late_await(RS_LATE)
        rows_all = plane * 8
        chosen = lanes(8, rows_all) % 8 == lax.broadcasted_iota(jnp.int32, (8, rows_all), 0)
        total = mm(jnp.where(chosen, 1.0, 0.0).astype(BF16), late.at[1].reshape(rows_all, 128)[...])
        z_send[...] = total
        z_recv[my_z] = total
        for copy in z_copies():
            copy.start()

    def late_finish():
        others = z_recv.at[pl.ds(0, NZ - 1)]
        pltpu.make_async_copy(others, others, snap_r.at[1]).wait()
        total = z_recv[0]
        for k in range(1, NZ):
            total = total + z_recv[k]
        piece_l[...] = total.astype(BF16)
        late_send(AG_LATE, lambda place: piece_l)

    def late_tile(tile):
        return late.at[2].reshape(plane * 8, 128)[tile * 64 : tile * 64 + 64, :]

    def arrived(hop):
        dst = recv_buf(hop)
        got = [dst.at[part].reshape(halo, 128)[...] for part in range(dst.shape[0])]
        return got[0] if len(got) == 1 else jnp.concatenate(got, axis=1)

    def far(got):
        both = mm(sw[...], got)
        low = lanes(width, got.shape[1]) % 128 < 64
        return jnp.where(low, both[:width, :], both[width:, :])

    def onward(got, composed):
        rows = mm(composed[...], got)
        return jnp.where(lanes(halo, 128) < 64, rows[halo:, :], rows[:halo, :])

    start = jnp.concatenate([held[...], extra], axis=1)
    launch(0, to_send(start.astype(BF16)))

    wts = [columns[:, 8 + d : 9 + d] for d in range(degs)]
    srcs = [columns[:, d : d + 1].astype(jnp.int32) for d in range(degs)]
    for first in range(0, width, 128):
        here = lanes(128, width + halo)
        total = jnp.zeros((128, width + halo), F32)
        for d in range(degs):
            total = total + jnp.where(srcs[d][first : first + 128] == here, wts[d][first : first + 128], 0.0)
        total = total.astype(BF16)
        wl[first : first + 128, :] = total[:, :width]
        sw[width + first : width + first + 128, :] = total[:, width:]
    deg_near = []
    for first in range(0, width, 128):
        block = push_block(first, 128)
        ml[first : first + 128, :] = block.astype(BF16)
        deg_near.append(jnp.sum(block, axis=1, keepdims=True))
    deg_near = jnp.concatenate(deg_near, axis=0)
    sw[:width, :] = jnp.where(
        lax.broadcasted_iota(jnp.int32, (width, halo), 0) == sr_ref[...], 1.0, 0.0
    ).astype(BF16)
    deg_in = wts[0]
    for d in range(1, degs):
        deg_in = deg_in + wts[d]
    inv_in = 1.0 / deg_in

    cols = gw_ref.shape[0]
    pick[...] = jnp.where(
        lax.broadcasted_iota(jnp.int32, (cols, 512), 0) == forward_map(lanes(1, 512), chans, fin), 1.0, 0.0
    ).astype(BF16)
    column = lax.broadcasted_iota(jnp.int32, (512, 1), 0)
    back_pick[...] = jnp.where(lanes(512, cols) == forward_map(column, chans, fin), 1.0, 0.0).astype(BF16)
    adjoint_pick = jnp.where(
        lanes(384, cols) == backward_map(column[:384], chans, fin), 1.0, 0.0
    ).astype(BF16)
    gate_w = gw_ref[...]
    cand_w = cw_ref[...]
    gate_f = mm(back_pick[...], gate_w)
    turned = pltpu.roll(gate_f, 64, 1)
    low512 = lanes(512, 128) < 64
    wg[:, :128] = jnp.where(low512, gate_f, turned).astype(BF16)
    wg[:, 128:] = jnp.where(low512, turned, gate_f).astype(BF16)
    wc[...] = mm_t1(back_pick[...], jnp.concatenate([cand_w, cand_w], axis=0)).astype(BF16)
    bg[...] = jnp.transpose(mm(adjoint_pick, gate_w)).astype(BF16)
    bc[:64, :] = mm_t1(cand_w, adjoint_pick).astype(BF16)
    bc[64:, :] = jnp.zeros((64, 384), BF16)
    bias2[0:1, :64] = cb_ref[...]
    bias2[0:1, 64:] = cb_ref[...]

    wide[...] = near(start.astype(BF16))
    await_recv(0)
    raw = far(arrived(0))
    deg_out = deg_near + raw[:, 128 + fin : 129 + fin] + raw[:, 129 + fin : 130 + fin]
    raw = raw + wide[...]
    inv_out = 1.0 / deg_out
    scale_f[...] = jnp.where(low128, inv_out, inv_in)
    scale_a[...] = jnp.where(low128, inv_in, inv_out)
    first_main = (raw[:, :128] * scale_f[...]).astype(BF16)
    states[:, :128] = first_main
    first_extra = jnp.where(lane128 % 64 < fin, raw[:, 128:] * scale_f[...], 0.0)
    second_in = jnp.concatenate([first_main, first_extra.astype(BF16)], axis=1)
    launch(1, to_send(second_in))
    for comp, times, by_push, by_pull in ((comp_f, 1.0, inv_out, inv_in), (comp_a, 2.0, inv_in, inv_out)):
        pushed = (sw[:width, :].astype(F32) * by_push).astype(BF16)
        pulled = (sw[width:, :].astype(F32) * by_pull).astype(BF16)
        comp[halo:, :] = (mm(sp[halo:, :], pushed) * times).astype(BF16)
        comp[:halo, :] = (mm(sp[:halo, :], pulled) * times).astype(BF16)
    ones = jnp.where(
        low128, held[...], jnp.where(lane128 < 64 + fin, extra, jnp.where(lane128 == 64 + fin, 1.0, 0.0))
    )
    states[:, 256:384] = ones.astype(BF16)
    wide[...] = near(second_in)
    bias = jnp.broadcast_to(gb_ref[...], (width, 128))
    turned = pltpu.roll(bias, 64, 1)
    local[...] = (
        mm(states[:, :128], wg[:128, :128])
        + mm(states[:, 256:384], wg[256:384, :128])
        + jnp.where(low128, bias, turned)
    )
    await_recv(1)
    raw = far(arrived(1)) + wide[...]
    states[:, 128:256] = (2.0 * raw[:, :128] * scale_f[...] - held[...]).astype(BF16)
    second_extra = 2.0 * raw[:, 128:] * scale_f[...] - extra
    tail = first_extra.astype(BF16).astype(F32) + pltpu.roll(second_extra.astype(BF16).astype(F32), fin, 1)
    states[:, 384:] = tail.astype(BF16)

    reset = jax.nn.sigmoid(
        local[...] + mm(states[:, 128:256], wg[128:256, :128]) + mm(states[:, 384:], wg[384:, :128])
    )
    scaled = (reset * held[...]).astype(BF16)
    launch(2, to_send(scaled))
    beside = near(scaled)
    local[...] = beside
    ahead[...] = to_send((beside * scale_f[...]).astype(BF16))
    update = jax.nn.sigmoid(mm(states[...], wg[:, 128:]) + jnp.where(low128, turned, bias))
    gate_r[...] = reset
    gate_u[...] = update
    slope_c[...] = upward[...] * (1.0 - update)
    slope_r[...] = held[...] * reset * (1.0 - reset)
    mixed[:, 256:384] = jnp.where(low128, scaled, states[:, 256:384])
    mixed[:, 384:] = states[:, 384:]
    await_recv(2)
    got = arrived(2)
    launch(3, ahead[...] + onward(got, comp_f))
    hop_one = ((far(got) + local[...]) * scale_f[...]).astype(BF16)
    mixed[:, :128] = hop_one
    local[...] = near(hop_one)
    part[...] = (
        mm(mixed[:, :128], wc[:128, :]) + mm(mixed[:, 256:], wc[256:, :]) + bias2[0:1, :]
    )
    await_recv(3)
    raw = far(arrived(3)) + local[...]
    mixed[:, 128:256] = (2.0 * raw * scale_f[...] - scaled.astype(F32)).astype(BF16)
    cand = jnp.tanh(part[...] + mm(mixed[:, 128:256], wc[128:256, :]))
    cand_grad = (slope_c[...] * (1.0 - cand * cand)).astype(BF16)

    def outer_hop(grad, weights, hop):
        outer = mm(grad, weights[:, :128])
        values = (outer * scale_a[...]).astype(BF16)
        launch(hop, to_send(values))
        return outer, values

    def inner_hop(grad, weights, hop, outer, values, meanwhile):
        beside = near(values)
        local[...] = beside
        inner = mm(grad, weights[:, 128:256])
        inner_v[...] = inner
        ahead[...] = to_send(((inner + 2.0 * beside) * scale_a[...]).astype(BF16))
        field[...] = mm(grad, weights[:, 256:384]) - outer - pltpu.roll(outer, 64, 1)
        meanwhile()
        await_recv(hop)
        got = arrived(hop)
        launch(hop + 1, ahead[...] + onward(got, comp_a))
        raw = far(got) + local[...]
        values = ((inner_v[...] + 2.0 * raw) * scale_a[...]).astype(BF16)
        local[...] = near(values)

    def last_hop(hop):
        await_recv(hop)
        raw = far(arrived(hop)) + local[...]
        return field[...] + raw + pltpu.roll(raw, 64, 1)

    def early_sums():
        update_part = upward[...] * (held[...] - cand) * gate_u[...] * (1.0 - gate_u[...])
        part[...] = update_part
        grads = turn(jnp.where(low128, cand_grad.astype(F32), update_part)).astype(BF16)
        by_cand = mm(grads[:64, :], mixed[...])
        by_update = mm(grads[64:, :], states[...])
        for tile in range(4):
            dst = early.at[0, tile // 2].reshape(halo, 128)
            at = tile % 2 * 128
            dst[at : at + 64, :] = by_cand[:, tile * 128 : tile * 128 + 128].astype(BF16)
            dst[at + 64 : at + 128, :] = by_update[:, tile * 128 : tile * 128 + 128].astype(BF16)
        send_all(RS_EARLY)

    outer, values = outer_hop(cand_grad, bc, 4)
    inner_hop(cand_grad, bc, 4, outer, values, early_sums)
    reduce_pieces(RS_EARLY, 0)
    scaled_grad = last_hop(5)
    gate_grad = jnp.where(low128, scaled_grad * slope_r[...], part[...]).astype(BF16)
    by_reset = mm(turn(gate_grad)[:64, :].astype(BF16), states[...])
    for tile in range(4):
        late.at[0].reshape(plane * 8, 128)[tile * 64 : tile * 64 + 64, :] = by_reset[
            :, tile * 128 : tile * 128 + 128
        ].astype(BF16)
    late_send(RS_LATE, lambda place: late.at[0, place])
    outer, values = outer_hop(gate_grad, bg, 6)
    finish_pieces(AG_EARLY, 0, piece_e)
    part[...] = upward[...] * gate_u[...] + scaled_grad * gate_r[...]
    inner_hop(gate_grad, bg, 6, outer, values, late_reduce)
    field[...] = field[...] + part[...]
    late_finish()

    await_recv(AG_EARLY)
    bias_row = jnp.where(lanes(8, 128) == 64 + fin, 1.0, 0.0).astype(BF16)

    def put_bias(tiles, bias_out):
        bias_out[...] = mm_t1(bias_row, tiles[2])[0:1, :] * factor

    tiles = [gathered(tile)[:64] for tile in range(4)]
    total = mm(tiles[0], back_pick[:128, :])
    for tile in range(1, 4):
        total = total + mm(tiles[tile], back_pick[tile * 128 : tile * 128 + 128, :])
    cand_out[...] = total * factor
    put_bias(tiles, cand_bias_out)
    state_ref[0] = jnp.transpose(last_hop(7))[:64, :].astype(BF16)
    late_await(AG_LATE)
    tiles = [
        jnp.concatenate([late_tile(tile), gathered(tile)[64:]], axis=0)
        for tile in range(4)
    ]
    total = mm_t1(pick[:, :128], tiles[0])
    for tile in range(1, 4):
        total = total + mm_t1(pick[:, tile * 128 : tile * 128 + 128], tiles[tile])
    gate_out[...] = total * factor
    put_bias(tiles, gate_bias_out)

    for group in range(RS_LATE):
        rest = recv_buf(group).at[:, pl.ds(0, n_dom - 1)]
        pltpu.make_async_copy(rest, rest, ssem.at[group]).wait()
    for group in (RS_LATE, AG_LATE):
        rest = late.at[2, pl.ds(0, plane - 1)]
        pltpu.make_async_copy(rest, rest, ssem.at[group]).wait()
    others = snap_recv.at[0, pl.ds(0, n_snap - 1)]
    pltpu.make_async_copy(others, others, snap_s.at[0]).wait()
    others = z_recv.at[pl.ds(0, NZ - 1)]
    pltpu.make_async_copy(others, others, snap_s.at[1]).wait()


def solution(mesh):
    n_dom, n_snap = mesh.shape["dom"], mesh.shape["snap"]

    def body(readings, previous, upstream, gw, gb, cw, cb, nb, ew, sr):
        fin, hidden, width = readings.shape[1], previous.shape[1], readings.shape[2]
        chans, halo = fin + hidden, sr.shape[1]
        slots = halo // n_dom
        vmem = pl.BlockSpec(memory_space=pltpu.VMEM)

        factor = 1.0 / math.sqrt(readings.shape[0] * n_snap * width * n_dom)

        def run(*refs):
            kernel(n_dom, n_snap, width, fin, chans, halo, factor, *refs)

        cols = gw.shape[1]
        arrays = (readings, previous, upstream, gw.T, gb.reshape(1, -1), cw, cb.reshape(1, -1), nb, ew, sr)
        state, gate, gate_b, cand, cand_b = pl.pallas_call(
            run,
            out_shape=(
                jax.ShapeDtypeStruct((1, hidden, width), BF16),
                jax.ShapeDtypeStruct((cols, 2 * hidden), F32),
                jax.ShapeDtypeStruct((1, 2 * hidden), F32),
                jax.ShapeDtypeStruct((hidden, cols), F32),
                jax.ShapeDtypeStruct((1, hidden), F32),
            ),
            in_specs=[pl.BlockSpec(memory_space=pl.ANY)] * 10,
            out_specs=(vmem,) * 5,
            scratch_shapes=[
                pltpu.VMEM((2 * halo, width), BF16),
                pltpu.VMEM((width, width), BF16),
                pltpu.VMEM((width, width), BF16),
                pltpu.VMEM((2 * width, halo), BF16),
                pltpu.VMEM((2 * halo, halo), BF16),
                pltpu.VMEM((2 * halo, halo), BF16),
                pltpu.VMEM((width, 128), F32),
                pltpu.VMEM((width, 128), F32),
                pltpu.VMEM((width, 128), F32),
                pltpu.VMEM((width, 128), F32),
                pltpu.VMEM((width, 128), F32),
                pltpu.VMEM((width, 256), F32),
                pltpu.VMEM((width, 512), BF16),
                pltpu.VMEM((width, 512), BF16),
                pltpu.VMEM((width, 128), F32),
                pltpu.VMEM((512, 256), BF16),
                pltpu.VMEM((512, 128), BF16),
                pltpu.VMEM((128, 384), BF16),
                pltpu.VMEM((128, 384), BF16),
                pltpu.VMEM((2, 2, n_dom, slots, 128), BF16),
                pltpu.VMEM((2, 2, n_dom, slots, 128), BF16),
                pltpu.VMEM((HOPS - 2, 1, n_dom, slots, 128), BF16),
                pltpu.VMEM((HOPS - 2, 1, n_dom, slots, 128), BF16),
                pltpu.SemaphoreType.DMA((GROUPS,)),
                pltpu.SemaphoreType.DMA((GROUPS,)),
                pltpu.SemaphoreType.DMA((GROUPS,)),
                pltpu.VMEM((2, 128, width), F32),
                pltpu.VMEM((3, 2, n_dom, slots, 128), BF16),
                pltpu.VMEM((3, n_snap * NY * NC, 8, 128), BF16),
                pltpu.VMEM((2, slots, 128), BF16),
                pltpu.VMEM((8, 128), BF16),
                pltpu.VMEM((2, 8, 128), F32),
                pltpu.VMEM((2, n_snap, 8, 128), F32),
                pltpu.SemaphoreType.DMA((2,)),
                pltpu.SemaphoreType.DMA((2,)),
                pltpu.VMEM((512, cols), BF16),
                pltpu.VMEM((cols, 512), BF16),
                pltpu.VMEM((8, 128), F32),
                *[pltpu.VMEM((width, 128), F32)] * 6,
                pltpu.VMEM((halo, 128), F32),
                pltpu.VMEM((8, 128), F32),
                pltpu.VMEM((NZ, 8, 128), F32),
                *(pltpu.VMEM(array.shape, array.dtype) for array in arrays),
                pltpu.SemaphoreType.DMA((len(arrays),)),
            ],
            compiler_params=pltpu.CompilerParams(collective_id=0, has_side_effects=True),
        )(*arrays)
        results = (state, gate, gate_b, cand, cand_b)

        def write(*refs):
            for src, dst in zip(refs[: len(results)], refs[len(results) :]):
                dst[...] = src[...]

        state, gate, gate_b, cand, cand_b = pl.pallas_call(
            write,
            out_shape=tuple(jax.ShapeDtypeStruct(array.shape, array.dtype) for array in results),
            in_specs=[vmem] * len(results),
            out_specs=(vmem,) * len(results),
        )(*results)
        return state, gate.T, gate_b.reshape(-1), cand, cand_b.reshape(-1)

    in_specs = (
        P("snap", None, "dom"), P("snap", None, "dom"), P("snap", None, "dom"),
        P(), P(), P(), P(), P(None, "dom"), P(None, "dom"), P("dom", None),
    )
    out_specs = (P("snap", None, "dom"), P(), P(), P(), P())
    return jax.shard_map(body, mesh=mesh, in_specs=in_specs, out_specs=out_specs, check_vma=False)
```

```python
import math

import jax
import jax.numpy as jnp
from jax import lax
from jax.experimental import pallas as pl
from jax.experimental.pallas import tpu as pltpu
from jax.sharding import PartitionSpec as P

F32, BF16 = jnp.float32, jnp.bfloat16
MESH = pl.DeviceIdType.MESH
HOPS = 8
RS_EARLY, AG_EARLY, RS_LATE, AG_LATE, GROUPS = 8, 9, 10, 11, 12
NY, NZ, NC = 4, 8, 2


def mm(a, b):
    return jnp.dot(a, b, preferred_element_type=F32)


def mm_t1(a, b):
    return lax.dot_general(a, b, (((1,), (1,)), ((), ())), preferred_element_type=F32)


def turn(a):
    return jnp.transpose(a.astype(F32))


def lanes(rows, width):
    return lax.broadcasted_iota(jnp.int32, (rows, width), 1)


def forward_map(lane, chans, fin):
    tile, at = lane // 128, lane % 128
    upper, low = at >= 64, at % 64
    first = jnp.where(upper, 3 * chans, chans) + fin + low
    second = jnp.where(upper, 4 * chans, 2 * chans) + fin + low
    third = jnp.where(upper, jnp.where(low < fin, low, -1), fin + low)
    order = jnp.where(upper, 3, 1) + low // fin
    fourth = jnp.where(low < 2 * fin, order * chans + low % fin, -1)
    return jnp.where(tile == 0, first, jnp.where(tile == 1, second, jnp.where(tile == 2, third, fourth)))


def backward_map(lane, chans, fin):
    tile, at = lane // 128, lane % 128
    upper, low = at >= 64, at % 64
    order = jnp.where(
        tile == 0, jnp.where(upper, 2, 4), jnp.where(tile == 1, jnp.where(upper, 1, 3), 0)
    )
    return order * chans + fin + low


def kernel(
    n_dom, n_snap, width, fin, chans, halo, factor,
    *refs,
):
    sources, refs = refs[:10], refs[10:]
    landed, refs = refs[-11:-1], refs[:-11] + refs[-1:]
    copies = [
        pltpu.make_async_copy(src, dst, refs[-1].at[at]) for at, (src, dst) in enumerate(zip(sources, landed))
    ]
    for copy in copies:
        copy.start()
    step(n_dom, n_snap, width, fin, chans, halo, factor, copies, *landed, *refs[:-1])


def step(
    n_dom, n_snap, width, fin, chans, halo, factor, copies,
    readings_ref, previous_ref, upstream_ref, gw_ref, gb_ref, cw_ref, cb_ref, nb_ref, ew_ref, sr_ref,
    state_ref, gate_out, gate_bias_out, cand_out, cand_bias_out,
    sp, ml, wl, sw, comp_f, comp_a, held, upward, scale_f, scale_a, local, wide, states, mixed, field, wg, wc, bg, bc,
    send_w, recv_w, send_n, recv_n, ssem, rsem, osem, rows,
    early, late, piece_e, piece_l, z_send_e, z_recv_e, snap_s, snap_r, back_pick, pick, bias2,
    gate_r, gate_u, slope_c, slope_r, part, inner_v, ahead, z_send, z_recv,
):
    me = lax.axis_index("dom")
    barrier = pltpu.get_barrier_semaphore()

    my_core, my_z, my_y = me % NC, me // NC % NZ, me // (NC * NZ)

    def each_peer(visit):
        def ring(t, c):
            z = (my_z + NZ + NZ // 2 + (t + 1) // 2 * (1 - t % 2 * 2)) % NZ
            for dy in (2, 1, 3, 0):
                for dc in range(NC):
                    visit(((my_y + dy) % NY * NZ + z) * NC + (my_core + dc) % NC)
            return c

        lax.fori_loop(0, NZ - 1, ring, 0)
        for dy in (2, 1, 3, 0):
            for dc in range(NC):
                if dy or dc:
                    visit(((my_y + dy) % NY * NZ + my_z) * NC + (my_core + dc) % NC)

    each_peer(lambda peer: pl.semaphore_signal(barrier, inc=1, device_id={"dom": peer}, device_id_type=MESH))
    mine = lax.axis_index("snap")
    plane = n_snap * NY * NC
    my_place = (mine * NY + my_y) * NC + my_core

    def each_mate(visit):
        for dx in (2, 1, 3, 0):
            for dy in (2, 1, 3, 0):
                for dc in range(NC):
                    if dx or dy or dc:
                        x, y, c = (mine + dx) % n_snap, (my_y + dy) % NY, (my_core + dc) % NC
                        visit((x * NY + y) * NC + c, {"snap": x, "dom": (y * NZ + my_z) * NC + c})

    for dx in range(1, n_snap):
        for dy in range(NY):
            for dc in range(NC):
                x, y, c = (mine + dx) % n_snap, (my_y + dy) % NY, (my_core + dc) % NC
                pl.semaphore_signal(
                    barrier, inc=1, device_id={"snap": x, "dom": (y * NZ + my_z) * NC + c}, device_id_type=MESH
                )

    for copy in copies:
        copy.wait()
    lane128 = lanes(width, 128)
    low128 = lane128 < 64

    prev = previous_ref[0].astype(F32)
    held[...] = jnp.transpose(jnp.concatenate([prev, prev], axis=0))
    ups = upstream_ref[0].astype(F32)
    upward[...] = jnp.transpose(jnp.concatenate([ups, ups], axis=0))
    read = readings_ref[0].astype(F32)
    degs = nb_ref.shape[0]
    rows[...] = jnp.zeros_like(rows)
    rows[0, 0:fin, :] = read
    rows[0, 64 : 64 + fin, :] = read
    rows[1, 0:degs, :] = nb_ref[...].astype(F32)
    rows[1, 8 : 8 + degs, :] = ew_ref[...]
    rows[1, 16:17, :halo] = sr_ref[...].astype(F32)
    extra = jnp.transpose(rows[0])
    columns = jnp.transpose(rows[1])

    rows_sel = columns[:halo, 16:17].astype(jnp.int32)
    sp[:halo, :] = jnp.where(lanes(halo, width) == rows_sel, 1.0, 0.0).astype(BF16)

    def push_block(first, rows):
        here = lax.broadcasted_iota(jnp.int32, (rows, width), 0) + first
        total = jnp.zeros((rows, width), F32)
        for d in range(degs):
            total = total + jnp.where(nb_ref[d : d + 1, :] == here, ew_ref[d : d + 1, :], 0.0)
        return total

    edge_sums = push_block(width, halo)
    sp[halo:, :] = edge_sums.astype(BF16)
    deg_halo = jnp.sum(edge_sums, axis=1, keepdims=True)
    deg_high = deg_halo.astype(BF16).astype(F32)
    deg_rest = deg_halo - deg_high

    def send_buf(hop):
        return send_w.at[hop] if hop < 2 else send_n.at[hop - 2]

    def recv_buf(hop):
        return recv_w.at[hop] if hop < 2 else recv_n.at[hop - 2]

    def send_all(group):
        src, dst = send_buf(group), recv_buf(group)

        def go(peer):
            pltpu.make_async_remote_copy(
                src.at[:, peer], dst.at[:, me], ssem.at[group], rsem.at[group],
                device_id={"dom": peer}, device_id_type=MESH,
            ).start()

        each_peer(go)
        pltpu.make_async_copy(src.at[:, me], dst.at[:, me], osem.at[group]).start()

    def to_send(values):
        rows = mm(sp[...], values)
        return jnp.where(lanes(halo, values.shape[1]) % 128 < 64, rows[halo:, :], rows[:halo, :])

    def launch(hop, out):
        span = out.shape[1]
        if hop == 0:
            lane = lanes(halo, span)
            out = jnp.where(lane == 128 + fin, deg_high, jnp.where(lane == 128 + fin + 1, deg_rest, out))
        out = out.astype(BF16)
        src = send_buf(hop)
        for part in range(span // 128):
            src.at[part].reshape(halo, 128)[...] = out[:, part * 128 : part * 128 + 128]

        if hop == 0:
            pl.semaphore_wait(barrier, n_dom - 1 + (n_snap - 1) * NY * NC)
        send_all(hop)

    def near(values):
        low = lanes(*values.shape) % 128 < 64
        return jnp.where(low, mm(ml[...], values), mm(wl[...], values))

    def await_recv(hop):
        dst = recv_buf(hop)
        rest = dst.at[:, pl.ds(0, n_dom - 1)]
        pltpu.make_async_copy(rest, rest, rsem.at[hop]).wait()
        pltpu.make_async_copy(dst.at[:, me], dst.at[:, me], osem.at[hop]).wait()

    def tile_rows(buf, tile, count):
        return buf.at[2].reshape(plane * buf.shape[2], 128)[tile * count : tile * count + count, :]

    def plane_send(group, buf, slot, piece_of):
        dst = buf.at[slot]

        def go(place, device):
            pltpu.make_async_remote_copy(
                piece_of(place), dst.at[my_place], ssem.at[group], rsem.at[group],
                device_id=device, device_id_type=MESH,
            ).start()

        each_mate(go)
        pltpu.make_async_copy(piece_of(my_place), dst.at[my_place], osem.at[group]).start()

    def plane_await(group, buf, slot):
        dst = buf.at[slot]
        rest = dst.at[pl.ds(0, plane - 1)]
        pltpu.make_async_copy(rest, rest, rsem.at[group]).wait()
        pltpu.make_async_copy(dst.at[my_place], dst.at[my_place], osem.at[group]).wait()

    def reduce_pieces(group, buf, which, mine_z, all_z):
        plane_await(group, buf, 1)
        height = buf.shape[2]
        rows_all = plane * height
        chosen = lanes(height, rows_all) % height == lax.broadcasted_iota(jnp.int32, (height, rows_all), 0)
        total = mm(jnp.where(chosen, 1.0, 0.0).astype(BF16), buf.at[1].reshape(rows_all, 128)[...])
        mine_z[...] = total
        all_z[my_z] = total
        for dz in (4, 3, 5, 2, 6, 1, 7):
            pltpu.make_async_remote_copy(
                mine_z, all_z.at[my_z], snap_s.at[which], snap_r.at[which],
                device_id={"dom": (my_y * NZ + (my_z + dz) % NZ) * NC + my_core}, device_id_type=MESH,
            ).start()

    def finish_pieces(group, buf, which, all_z, piece):
        others = all_z.at[pl.ds(0, NZ - 1)]
        pltpu.make_async_copy(others, others, snap_r.at[which]).wait()
        total = all_z[0]
        for k in range(1, NZ):
            total = total + all_z[k]
        piece[...] = total.astype(BF16)
        plane_send(group, buf, 2, lambda place: piece)


    def arrived(hop):
        dst = recv_buf(hop)
        got = [dst.at[part].reshape(halo, 128)[...] for part in range(dst.shape[0])]
        return got[0] if len(got) == 1 else jnp.concatenate(got, axis=1)

    def far(got):
        both = mm(sw[...], got)
        low = lanes(width, got.shape[1]) % 128 < 64
        return jnp.where(low, both[:width, :], both[width:, :])

    def onward(got, composed):
        rows = mm(composed[...], got)
        return jnp.where(lanes(halo, 128) < 64, rows[halo:, :], rows[:halo, :])

    start = jnp.concatenate([held[...], extra], axis=1)
    launch(0, to_send(start.astype(BF16)))

    wts = [columns[:, 8 + d : 9 + d] for d in range(degs)]
    srcs = [columns[:, d : d + 1].astype(jnp.int32) for d in range(degs)]
    for first in range(0, width, 128):
        here = lanes(128, width + halo)
        total = jnp.zeros((128, width + halo), F32)
        for d in range(degs):
            total = total + jnp.where(srcs[d][first : first + 128] == here, wts[d][first : first + 128], 0.0)
        total = total.astype(BF16)
        wl[first : first + 128, :] = total[:, :width]
        sw[width + first : width + first + 128, :] = total[:, width:]
    deg_near = []
    for first in range(0, width, 128):
        block = push_block(first, 128)
        ml[first : first + 128, :] = block.astype(BF16)
        deg_near.append(jnp.sum(block, axis=1, keepdims=True))
    deg_near = jnp.concatenate(deg_near, axis=0)
    sw[:width, :] = jnp.where(
        lax.broadcasted_iota(jnp.int32, (width, halo), 0) == sr_ref[...], 1.0, 0.0
    ).astype(BF16)
    deg_in = wts[0]
    for d in range(1, degs):
        deg_in = deg_in + wts[d]
    inv_in = 1.0 / deg_in

    cols = gw_ref.shape[0]
    pick[...] = jnp.where(
        lax.broadcasted_iota(jnp.int32, (cols, 512), 0) == forward_map(lanes(1, 512), chans, fin), 1.0, 0.0
    ).astype(BF16)
    column = lax.broadcasted_iota(jnp.int32, (512, 1), 0)
    back_pick[...] = jnp.where(lanes(512, cols) == forward_map(column, chans, fin), 1.0, 0.0).astype(BF16)
    adjoint_pick = jnp.where(
        lanes(384, cols) == backward_map(column[:384], chans, fin), 1.0, 0.0
    ).astype(BF16)
    gate_w = gw_ref[...]
    cand_w = cw_ref[...]
    gate_f = mm(back_pick[...], gate_w)
    turned = pltpu.roll(gate_f, 64, 1)
    low512 = lanes(512, 128) < 64
    wg[:, :128] = jnp.where(low512, gate_f, turned).astype(BF16)
    wg[:, 128:] = jnp.where(low512, turned, gate_f).astype(BF16)
    wc[...] = mm_t1(back_pick[...], jnp.concatenate([cand_w, cand_w], axis=0)).astype(BF16)
    bg[...] = jnp.transpose(mm(adjoint_pick, gate_w)).astype(BF16)
    bc[:64, :] = mm_t1(cand_w, adjoint_pick).astype(BF16)
    bc[64:, :] = jnp.zeros((64, 384), BF16)
    bias2[0:1, :64] = cb_ref[...]
    bias2[0:1, 64:] = cb_ref[...]

    wide[...] = near(start.astype(BF16))
    await_recv(0)
    raw = far(arrived(0))
    deg_out = deg_near + raw[:, 128 + fin : 129 + fin] + raw[:, 129 + fin : 130 + fin]
    raw = raw + wide[...]
    inv_out = 1.0 / deg_out
    scale_f[...] = jnp.where(low128, inv_out, inv_in)
    scale_a[...] = jnp.where(low128, inv_in, inv_out)
    first_main = (raw[:, :128] * scale_f[...]).astype(BF16)
    states[:, :128] = first_main
    first_extra = jnp.where(lane128 % 64 < fin, raw[:, 128:] * scale_f[...], 0.0)
    second_in = jnp.concatenate([first_main, first_extra.astype(BF16)], axis=1)
    launch(1, to_send(second_in))
    for comp, times, by_push, by_pull in ((comp_f, 1.0, inv_out, inv_in), (comp_a, 2.0, inv_in, inv_out)):
        pushed = (sw[:width, :].astype(F32) * by_push).astype(BF16)
        pulled = (sw[width:, :].astype(F32) * by_pull).astype(BF16)
        comp[halo:, :] = (mm(sp[halo:, :], pushed) * times).astype(BF16)
        comp[:halo, :] = (mm(sp[:halo, :], pulled) * times).astype(BF16)
    ones = jnp.where(
        low128, held[...], jnp.where(lane128 < 64 + fin, extra, jnp.where(lane128 == 64 + fin, 1.0, 0.0))
    )
    states[:, 256:384] = ones.astype(BF16)
    wide[...] = near(second_in)
    bias = jnp.broadcast_to(gb_ref[...], (width, 128))
    turned = pltpu.roll(bias, 64, 1)
    local[...] = (
        mm(states[:, :128], wg[:128, :128])
        + mm(states[:, 256:384], wg[256:384, :128])
        + jnp.where(low128, bias, turned)
    )
    await_recv(1)
    raw = far(arrived(1)) + wide[...]
    states[:, 128:256] = (2.0 * raw[:, :128] * scale_f[...] - held[...]).astype(BF16)
    second_extra = 2.0 * raw[:, 128:] * scale_f[...] - extra
    tail = first_extra.astype(BF16).astype(F32) + pltpu.roll(second_extra.astype(BF16).astype(F32), fin, 1)
    states[:, 384:] = tail.astype(BF16)

    reset = jax.nn.sigmoid(
        local[...] + mm(states[:, 128:256], wg[128:256, :128]) + mm(states[:, 384:], wg[384:, :128])
    )
    scaled = (reset * held[...]).astype(BF16)
    launch(2, to_send(scaled))
    beside = near(scaled)
    local[...] = beside
    ahead[...] = to_send((beside * scale_f[...]).astype(BF16))
    update = jax.nn.sigmoid(mm(states[...], wg[:, 128:]) + jnp.where(low128, turned, bias))
    gate_r[...] = reset
    gate_u[...] = update
    slope_c[...] = upward[...] * (1.0 - update)
    slope_r[...] = held[...] * reset * (1.0 - reset)
    mixed[:, 256:384] = jnp.where(low128, scaled, states[:, 256:384])
    mixed[:, 384:] = states[:, 384:]
    await_recv(2)
    got = arrived(2)
    launch(3, ahead[...] + onward(got, comp_f))
    hop_one = ((far(got) + local[...]) * scale_f[...]).astype(BF16)
    mixed[:, :128] = hop_one
    local[...] = near(hop_one)
    part[...] = (
        mm(mixed[:, :128], wc[:128, :]) + mm(mixed[:, 256:], wc[256:, :]) + bias2[0:1, :]
    )
    await_recv(3)
    raw = far(arrived(3)) + local[...]
    mixed[:, 128:256] = (2.0 * raw * scale_f[...] - scaled.astype(F32)).astype(BF16)
    cand = jnp.tanh(part[...] + mm(mixed[:, 128:256], wc[128:256, :]))
    cand_grad = (slope_c[...] * (1.0 - cand * cand)).astype(BF16)

    def outer_hop(grad, weights, hop):
        outer = mm(grad, weights[:, :128])
        values = (outer * scale_a[...]).astype(BF16)
        launch(hop, to_send(values))
        return outer, values

    def inner_hop(grad, weights, hop, outer, values, meanwhile):
        beside = near(values)
        local[...] = beside
        inner = mm(grad, weights[:, 128:256])
        inner_v[...] = inner
        ahead[...] = to_send(((inner + 2.0 * beside) * scale_a[...]).astype(BF16))
        field[...] = mm(grad, weights[:, 256:384]) - outer - pltpu.roll(outer, 64, 1)
        meanwhile()
        await_recv(hop)
        got = arrived(hop)
        launch(hop + 1, ahead[...] + onward(got, comp_a))
        raw = far(got) + local[...]
        values = ((inner_v[...] + 2.0 * raw) * scale_a[...]).astype(BF16)
        local[...] = near(values)

    def last_hop(hop):
        await_recv(hop)
        raw = far(arrived(hop)) + local[...]
        return field[...] + raw + pltpu.roll(raw, 64, 1)

    def early_sums():
        update_part = upward[...] * (held[...] - cand) * gate_u[...] * (1.0 - gate_u[...])
        part[...] = update_part
        grads = turn(jnp.where(low128, cand_grad.astype(F32), update_part)).astype(BF16)
        by_cand = mm(grads[:64, :], mixed[...])
        by_update = mm(grads[64:, :], states[...])
        for tile in range(4):
            dst = early.at[0].reshape(plane * 16, 128)
            at = tile * 128
            dst[at : at + 64, :] = by_cand[:, tile * 128 : tile * 128 + 128].astype(BF16)
            dst[at + 64 : at + 128, :] = by_update[:, tile * 128 : tile * 128 + 128].astype(BF16)
        plane_send(RS_EARLY, early, 1, lambda place: early.at[0, place])

    outer, values = outer_hop(cand_grad, bc, 4)
    inner_hop(cand_grad, bc, 4, outer, values, early_sums)
    reduce_pieces(RS_EARLY, early, 0, z_send_e, z_recv_e)
    scaled_grad = last_hop(5)
    gate_grad = jnp.where(low128, scaled_grad * slope_r[...], part[...]).astype(BF16)
    by_reset = mm(turn(gate_grad)[:64, :].astype(BF16), states[...])
    for tile in range(4):
        late.at[0].reshape(plane * 8, 128)[tile * 64 : tile * 64 + 64, :] = by_reset[
            :, tile * 128 : tile * 128 + 128
        ].astype(BF16)
    plane_send(RS_LATE, late, 1, lambda place: late.at[0, place])
    outer, values = outer_hop(gate_grad, bg, 6)
    finish_pieces(AG_EARLY, early, 0, z_recv_e, piece_e)
    part[...] = upward[...] * gate_u[...] + scaled_grad * gate_r[...]
    inner_hop(gate_grad, bg, 6, outer, values, lambda: reduce_pieces(RS_LATE, late, 1, z_send, z_recv))
    field[...] = field[...] + part[...]
    finish_pieces(AG_LATE, late, 1, z_recv, piece_l)

    plane_await(AG_EARLY, early, 2)
    bias_row = jnp.where(lanes(8, 128) == 64 + fin, 1.0, 0.0).astype(BF16)

    def put_bias(tiles, bias_out):
        bias_out[...] = mm_t1(bias_row, tiles[2])[0:1, :] * factor

    tiles = [tile_rows(early, tile, 128)[:64] for tile in range(4)]
    total = mm(tiles[0], back_pick[:128, :])
    for tile in range(1, 4):
        total = total + mm(tiles[tile], back_pick[tile * 128 : tile * 128 + 128, :])
    cand_out[...] = total * factor
    put_bias(tiles, cand_bias_out)
    state_ref[0] = jnp.transpose(last_hop(7))[:64, :].astype(BF16)
    plane_await(AG_LATE, late, 2)
    tiles = [
        jnp.concatenate([tile_rows(late, tile, 64), tile_rows(early, tile, 128)[64:]], axis=0)
        for tile in range(4)
    ]
    total = mm_t1(pick[:, :128], tiles[0])
    for tile in range(1, 4):
        total = total + mm_t1(pick[:, tile * 128 : tile * 128 + 128], tiles[tile])
    gate_out[...] = total * factor
    put_bias(tiles, gate_bias_out)

    for group in range(HOPS):
        rest = recv_buf(group).at[:, pl.ds(0, n_dom - 1)]
        pltpu.make_async_copy(rest, rest, ssem.at[group]).wait()
    for group, buf in ((RS_EARLY, early), (AG_EARLY, early), (RS_LATE, late), (AG_LATE, late)):
        rest = buf.at[2, pl.ds(0, plane - 1)]
        pltpu.make_async_copy(rest, rest, ssem.at[group]).wait()
    for which, all_z in ((0, z_recv_e), (1, z_recv)):
        others = all_z.at[pl.ds(0, NZ - 1)]
        pltpu.make_async_copy(others, others, snap_s.at[which]).wait()


def solution(mesh):
    n_dom, n_snap = mesh.shape["dom"], mesh.shape["snap"]

    def body(readings, previous, upstream, gw, gb, cw, cb, nb, ew, sr):
        fin, hidden, width = readings.shape[1], previous.shape[1], readings.shape[2]
        chans, halo = fin + hidden, sr.shape[1]
        slots = halo // n_dom
        vmem = pl.BlockSpec(memory_space=pltpu.VMEM)

        factor = 1.0 / math.sqrt(readings.shape[0] * n_snap * width * n_dom)

        def run(*refs):
            kernel(n_dom, n_snap, width, fin, chans, halo, factor, *refs)

        cols = gw.shape[1]
        arrays = (readings, previous, upstream, gw.T, gb.reshape(1, -1), cw, cb.reshape(1, -1), nb, ew, sr)
        state, gate, gate_b, cand, cand_b = pl.pallas_call(
            run,
            out_shape=(
                jax.ShapeDtypeStruct((1, hidden, width), BF16),
                jax.ShapeDtypeStruct((cols, 2 * hidden), F32),
                jax.ShapeDtypeStruct((1, 2 * hidden), F32),
                jax.ShapeDtypeStruct((hidden, cols), F32),
                jax.ShapeDtypeStruct((1, hidden), F32),
            ),
            in_specs=[pl.BlockSpec(memory_space=pl.ANY)] * 10,
            out_specs=(vmem,) * 5,
            scratch_shapes=[
                pltpu.VMEM((2 * halo, width), BF16),
                pltpu.VMEM((width, width), BF16),
                pltpu.VMEM((width, width), BF16),
                pltpu.VMEM((2 * width, halo), BF16),
                pltpu.VMEM((2 * halo, halo), BF16),
                pltpu.VMEM((2 * halo, halo), BF16),
                pltpu.VMEM((width, 128), F32),
                pltpu.VMEM((width, 128), F32),
                pltpu.VMEM((width, 128), F32),
                pltpu.VMEM((width, 128), F32),
                pltpu.VMEM((width, 128), F32),
                pltpu.VMEM((width, 256), F32),
                pltpu.VMEM((width, 512), BF16),
                pltpu.VMEM((width, 512), BF16),
                pltpu.VMEM((width, 128), F32),
                pltpu.VMEM((512, 256), BF16),
                pltpu.VMEM((512, 128), BF16),
                pltpu.VMEM((128, 384), BF16),
                pltpu.VMEM((128, 384), BF16),
                pltpu.VMEM((2, 2, n_dom, slots, 128), BF16),
                pltpu.VMEM((2, 2, n_dom, slots, 128), BF16),
                pltpu.VMEM((HOPS - 2, 1, n_dom, slots, 128), BF16),
                pltpu.VMEM((HOPS - 2, 1, n_dom, slots, 128), BF16),
                pltpu.SemaphoreType.DMA((GROUPS,)),
                pltpu.SemaphoreType.DMA((GROUPS,)),
                pltpu.SemaphoreType.DMA((GROUPS,)),
                pltpu.VMEM((2, 128, width), F32),
                pltpu.VMEM((3, n_snap * NY * NC, 16, 128), BF16),
                pltpu.VMEM((3, n_snap * NY * NC, 8, 128), BF16),
                pltpu.VMEM((16, 128), BF16),
                pltpu.VMEM((8, 128), BF16),
                pltpu.VMEM((16, 128), F32),
                pltpu.VMEM((NZ, 16, 128), F32),
                pltpu.SemaphoreType.DMA((2,)),
                pltpu.SemaphoreType.DMA((2,)),
                pltpu.VMEM((512, cols), BF16),
                pltpu.VMEM((cols, 512), BF16),
                pltpu.VMEM((8, 128), F32),
                *[pltpu.VMEM((width, 128), F32)] * 6,
                pltpu.VMEM((halo, 128), F32),
                pltpu.VMEM((8, 128), F32),
                pltpu.VMEM((NZ, 8, 128), F32),
                *(pltpu.VMEM(array.shape, array.dtype) for array in arrays),
                pltpu.SemaphoreType.DMA((len(arrays),)),
            ],
            compiler_params=pltpu.CompilerParams(collective_id=0, has_side_effects=True),
        )(*arrays)
        results = (state, gate, gate_b, cand, cand_b)

        def write(*refs):
            for src, dst in zip(refs[: len(results)], refs[len(results) :]):
                dst[...] = src[...]

        state, gate, gate_b, cand, cand_b = pl.pallas_call(
            write,
            out_shape=tuple(jax.ShapeDtypeStruct(array.shape, array.dtype) for array in results),
            in_specs=[vmem] * len(results),
            out_specs=(vmem,) * len(results),
        )(*results)
        return state, gate.T, gate_b.reshape(-1), cand, cand_b.reshape(-1)

    in_specs = (
        P("snap", None, "dom"), P("snap", None, "dom"), P("snap", None, "dom"),
        P(), P(), P(), P(), P(None, "dom"), P(None, "dom"), P("dom", None),
    )
    out_specs = (P("snap", None, "dom"), P(), P(), P(), P())
    return jax.shard_map(body, mesh=mesh, in_specs=in_specs, out_specs=out_specs, check_vma=False)
```
